32 devices in a mesh: grp: 2 (over x), ep: 8 (over z, y), sub: 2 (over core).
Axes of the slice: x: 2, y: 2, z: 4, core: 2. Of those that a mesh axis runs over, the one named last changes fastest.
Arguments:
- queries: bfloat16 [320, 16, 128], P(('grp', 'ep'), 'sub'), parts along dimension 0
- cache_keys: bfloat16 [320, 2, 384, 128], P(('grp', 'ep'), 'sub'), parts along dimension 0, may hold values from -6 to 6
- cache_values: bfloat16 [320, 2, 384, 128], P(('grp', 'ep'), 'sub'), parts along dimension 0, may hold values from -6 to 6
- new_keys: bfloat16 [320, 2, 128], P(('grp', 'ep'), 'sub'), parts along dimension 0
- new_values: bfloat16 [320, 2, 128], P(('grp', 'ep'), 'sub'), parts along dimension 0, may hold values from -6 to 6
- lengths: int32 [320], P(('grp', 'ep')), parts along dimension 0, may hold values from 1 to 384, as said below
- out_proj: bfloat16 [2048, 2048], P('sub'), may hold values from -1.5 to 1.5
- residual: bfloat16 [320, 2048], P(('grp', 'ep', 'sub')), parts along dimension 0, may hold values from -6 to 6
- norm_gain: float32 [2048], replicated, may hold values from 0.25 to 1.75
- gate_proj: bfloat16 [64, 2048, 768], P(('ep', 'sub')), may hold values from -0.125 to 0.125
- up_proj: bfloat16 [64, 2048, 768], P(('ep', 'sub')), may hold values from -0.125 to 0.125
- down_proj: bfloat16 [64, 768, 2048], P(('ep', 'sub')), may hold values from -0.21875 to 0.21875
- routing: int32 [320, 8], P(('grp', 'ep', 'sub')), parts along dimension 0, may hold values from 0 to 63, all different within a row; in each aligned block of 10 rows (0 to 9, 10 to 19, ...) at most 3 rows name the same one
- route_weights: float32 [320, 8], P(('grp', 'ep', 'sub')), parts along dimension 0, may hold values from 0.05 to 1
Outputs:
- layer_out: bfloat16 [320, 2048], P(('grp', 'ep', 'sub')), parts along dimension 0
The draws below stay inside these ranges and needn't reach their ends.
There are 2 independent parts, one for each index of `grp`. The reference program is written for one: setup_inputs(seed, part) draws one part's arguments, and reference() takes and returns one part's arrays. A program takes and returns all parts, laid end to end along the dimension named above; an argument that names none is the same for every part. Nothing has to cross between parts.
Inputs may be any that keep to these rules, and one draw needn't show every extreme that they name: Slots 0 to lengths - 1 of a request are live; some request has exactly 384. `routing`: each request names 8 different experts; among the 10 requests of one device no expert is named by more than 3, and some device reaches 3.
All inputs are finite; a program needn't handle non-finite values.
Results may differ from the reference program's by a relative error of at most 0.007.
Values may be sent and summed in bfloat16 or wider, within the bound.
No kernel may reach another device: no remote copies, remote signals or barrier semaphores. Data moves between devices by JAX's collectives and lax.ppermute only.
A program may use at most 128 MiB of HBM per device.

```python
import math
import jax
import jax.numpy as jnp
import numpy as np
from jax import lax

D = 2048
HD = 128
FF = 768
TOP = 8
HQ = 16
KVH = 2
EXPERTS = 64
WIN = 384
ROWS_DEV = 10
MOST = 3
ROWS = 160


def common_keys(key):
    base = jax.random.fold_in(key, 11)
    return jax.random.truncated_normal(base, -6.0, 6.0, (ROWS, KVH, WIN, HD), jnp.float32)


def draw_cache_keys(key, part):
    return common_keys(key).astype(jnp.bfloat16)


def draw_queries(key, part):
    values = jax.random.truncated_normal(jax.random.fold_in(key, 12), -6.0, 6.0, (ROWS, HQ, HD), jnp.float32)
    return values.astype(jnp.bfloat16)


def draw_new_keys(key, part):
    values = jax.random.truncated_normal(jax.random.fold_in(key, 13), -6.0, 6.0, (ROWS, KVH, HD), jnp.float32)
    return values.astype(jnp.bfloat16)


def draw_lengths(key, part):
    values = jax.random.randint(jax.random.fold_in(key, 14), (ROWS,), 1, WIN + 1, jnp.int32)
    return values.at[0].set(WIN)


def block_levels(stream_key, extent, shards, smallest, high):
    level, own = 1.0, jax.random.fold_in(stream_key, 6)
    for dim, parts in shards:
        heights = jnp.exp(jax.random.uniform(jax.random.fold_in(own, dim), (parts,), jnp.float32, smallest / len(shards), high / len(shards)))
        level = level * jnp.repeat(heights, extent[dim] // parts).reshape([-1 if axis == dim else 1 for axis in range(len(extent))])
    return level


def assign_block(rng, own, number, rows, number_of, top, bound, slope):
    sequence = jax.random.permutation(rng, number_of)
    packed, ordinary = portions_of(number_of, rows * top, bound, slope, True), portions_of(number_of, rows * top, bound, slope, False)
    places = jnp.arange(number_of)

    def named(tallies, rotation):
        used = int((tallies > 0).sum())
        fixed = max(1, used // 4)
        moved = fixed + (places - fixed + rotation * (used - fixed)) % max(1, number_of - fixed)
        return jnp.zeros((number_of,), jnp.int32).at[sequence[jnp.where(places < fixed, places, moved)]].set(jnp.asarray(tallies, jnp.int32))

    tallies = jnp.where(number % 4 == 0, named(packed, number // 4), named(ordinary, number - number // 4 - 1))
    mixed = jax.random.permutation(jax.random.fold_in(own, 3), number_of)
    source_of, taker = mixed[0:number_of // 2 * 2:2], mixed[1:number_of // 2 * 2:2]
    margin = jnp.minimum(tallies[source_of] - 1, bound - tallies[taker]) // 2
    margin = jnp.where((source_of == sequence[0]) | (taker == sequence[0]) | (tallies[taker] == 0), 0, jnp.maximum(margin, 0))
    moved = jax.random.randint(jax.random.fold_in(own, 4), (number_of // 2,), 0, 1 << 20) % (margin + 1)
    tallies = tallies.at[source_of].add(-moved).at[taker].add(moved)
    items = jnp.searchsorted(jnp.cumsum(tallies), jnp.arange(rows * top), side="right").astype(jnp.int32)
    table = items.reshape(top, rows).T
    table = table[jax.random.permutation(jax.random.fold_in(own, 1), rows)]
    rotation = jax.random.randint(jax.random.fold_in(own, 2), (rows, 1), 0, top)
    return jnp.take_along_axis(table, (jnp.arange(top)[None, :] + rotation) % top, axis=1)


def portions_of(count, total, reach, skew, full):
    weights = [(1 << 20) // math.isqrt(grade ** skew) + 1 for grade in range(1, count + 1)]
    largest = reach if full else min(reach, max(-(-total // count), total * weights[0] // sum(weights)))
    least = 1 if total - largest >= count - 1 else 0
    given, surplus = [largest] + [least] * (count - 1), total - largest - least * (count - 1)
    while surplus > 0:
        candidates = [i for i in range(1, count) if given[i] < largest] or [i for i in range(1, count) if given[i] < reach]
        whole, budget = sum([weights[i] for i in candidates]), surplus
        for i in candidates:
            more = min(reach - given[i], max(1, budget * weights[i] // whole), surplus)
            given[i] = given[i] + more
            surplus = surplus - more
    return np.array(given)


def centred(stream_key, extent, spread, most, split=(), held_as=jnp.bfloat16):
    result = spread * jax.random.normal(stream_key, extent, jnp.float32)
    if split:
        result = result * block_levels(stream_key, extent, split, -0.22, 0.18)
    return jnp.clip(result, -most, most).astype(held_as)


def setup_inputs(seed: int = 0, part: int = 0) -> dict:
    key_list = jax.random.split(jax.random.key(seed), 15)
    part_keys = jax.random.split(jax.random.fold_in(key_list[14], part), 15)
    queries = draw_queries(jax.random.fold_in(jax.random.fold_in(key_list[14], part), 71), part)
    cache_keys = draw_cache_keys(jax.random.fold_in(jax.random.fold_in(key_list[14], part), 71), part)
    cache_values = centred(part_keys[2], (ROWS, KVH, WIN, HD), 1.0, 6.0, ((0, 8), (1, 2)))
    new_keys = draw_new_keys(jax.random.fold_in(jax.random.fold_in(key_list[14], part), 71), part)
    new_values = centred(part_keys[4], (ROWS, KVH, HD), 1.0, 6.0, ((0, 8), (1, 2)))
    lengths = draw_lengths(jax.random.fold_in(jax.random.fold_in(key_list[14], part), 71), part)
    out_proj = centred(key_list[6], (HQ * HD, D), 0.25, 1.5, ((0, 2),))
    residual = centred(part_keys[7], (ROWS, D), 1.0, 6.0, ((0, 16),))
    norm_gain = jnp.clip(1.0 + 0.15 * jax.random.normal(key_list[8], (D,), jnp.float32), 0.25, 1.75)
    gate_proj = centred(key_list[9], (EXPERTS, D, FF), D ** -0.5, 0.125, ((0, 16),))
    up_proj = centred(key_list[10], (EXPERTS, D, FF), D ** -0.5, 0.125, ((0, 16),))
    down_proj = centred(key_list[11], (EXPERTS, FF, D), FF ** -0.5, 0.21875, ((0, 16),))
    routing_keys = jax.random.split(jax.random.fold_in(part_keys[12], 1), ROWS // ROWS_DEV)
    routing_turns = jax.random.permutation(jax.random.fold_in(part_keys[12], 3), ROWS // ROWS_DEV)
    routing = jax.vmap(lambda own, number: assign_block(jax.random.fold_in(part_keys[12], 2), own, number, ROWS_DEV, EXPERTS, TOP, MOST, 2))(routing_keys, routing_turns).reshape((ROWS, TOP))
    route_weights = jnp.clip(jnp.exp(math.log(1.0) - 2.9957323 * jax.random.uniform(part_keys[13], (ROWS, TOP), jnp.float32) ** block_levels(part_keys[13], (ROWS, TOP), ((0, 16),), -0.2, 0.2)), 0.05, 1.0)
    return {"queries": queries, "cache_keys": cache_keys, "cache_values": cache_values, "new_keys": new_keys, "new_values": new_values, "lengths": lengths, "out_proj": out_proj, "residual": residual, "norm_gain": norm_gain, "gate_proj": gate_proj, "up_proj": up_proj, "down_proj": down_proj, "routing": routing, "route_weights": route_weights}


def expert_block(operands):
    inputs, gate_mat, up_mat, down_mat = operands
    gate_val = jnp.dot(inputs, gate_mat, preferred_element_type=jnp.float32)
    up_val = jnp.dot(inputs, up_mat, preferred_element_type=jnp.float32)
    hidden = (jax.nn.silu(gate_val) * up_val).astype(jnp.bfloat16)
    return jnp.dot(hidden, down_mat, preferred_element_type=jnp.float32).astype(jnp.bfloat16)

def reference(queries, cache_keys, cache_values, new_keys, new_values, lengths, out_proj, residual, norm_gain, gate_proj, up_proj, down_proj, routing, route_weights):
    group_size = HQ // KVH
    score_scale = 1.0 / math.sqrt(HD)
    grouped = queries.astype(jnp.float32).reshape(ROWS, KVH, group_size, HD)
    scores = jnp.einsum('bgqd,bgjd->bgqj', grouped, cache_keys.astype(jnp.float32)) * score_scale
    own_score = jnp.einsum('bgqd,bgd->bgq', grouped, new_keys.astype(jnp.float32)) * score_scale
    valid_mask = jnp.arange(WIN, dtype=jnp.int32)[None, :] < lengths[:, None]
    scores = jnp.where(valid_mask[:, None, None, :], scores, -1e+30)
    top_score = jnp.maximum(lax.optimization_barrier(jnp.max(scores, -1)), own_score)
    weights = jnp.exp(scores - top_score[..., None])
    own_weight = jnp.exp(own_score - top_score)
    denominator = lax.optimization_barrier(jnp.sum(weights, -1)) + own_weight
    weights_low = lax.optimization_barrier(weights.astype(jnp.bfloat16)).astype(jnp.float32)
    own_low = lax.optimization_barrier(own_weight.astype(jnp.bfloat16)).astype(jnp.float32)
    mixture = jnp.einsum('bgqj,bgjd->bgqd', weights_low, cache_values.astype(jnp.float32))
    mixture = mixture + jnp.einsum('bgq,bgd->bgqd', own_low, new_values.astype(jnp.float32))
    head_out = (mixture / denominator[..., None]).reshape(ROWS, HQ * HD).astype(jnp.bfloat16)
    stream = residual.astype(jnp.float32) + jnp.dot(head_out, out_proj, preferred_element_type=jnp.float32)
    normed = (stream * lax.rsqrt(lax.optimization_barrier(jnp.mean(stream * stream, -1, keepdims=True)) + 1e-06) * norm_gain).astype(jnp.bfloat16)
    blocks = ROWS // ROWS_DEV
    chosen = (routing[:, :, None] == jnp.arange(EXPERTS, dtype=jnp.int32)[None, None, :]).astype(jnp.int32)
    expert_hits = lax.optimization_barrier(jnp.sum(chosen, 1)).reshape(blocks, ROWS_DEV, EXPERTS)
    earlier_hits = (jnp.cumsum(expert_hits, 1) - expert_hits).reshape(ROWS, EXPERTS)
    slot_rank = jnp.take_along_axis(earlier_hits, routing, 1).astype(jnp.int32)
    block_index = (jnp.arange(ROWS, dtype=jnp.int32) // ROWS_DEV)[:, None] + jnp.zeros((ROWS, TOP), jnp.int32)
    spread_rows = jnp.broadcast_to(normed[:, None, :], (ROWS, TOP, D))
    slotted = jnp.zeros((EXPERTS, blocks, MOST, D), jnp.bfloat16).at[routing, block_index, slot_rank].set(spread_rows)
    answered = lax.map(expert_block, (slotted.reshape(EXPERTS, blocks * MOST, D), gate_proj, up_proj, down_proj))
    answered = lax.optimization_barrier(answered.reshape(EXPERTS, blocks, MOST, D))
    picked_rows = answered[routing, block_index, slot_rank].astype(jnp.float32)
    expert_sum = lax.optimization_barrier(jnp.sum(route_weights[:, :, None] * picked_rows, 1))
    return (stream + expert_sum).astype(jnp.bfloat16)
```

```python
import functools
import math

import jax
import jax.numpy as jnp
from jax import lax
from jax.experimental import pallas as pl
from jax.experimental.pallas import tpu as pltpu
from jax.sharding import PartitionSpec as P

F32 = jnp.float32
BF16 = jnp.bfloat16
LANES = 128
SUBL = 8

VMEM = pl.BlockSpec(memory_space=pltpu.VMEM)
SMEM = pl.BlockSpec(memory_space=pltpu.SMEM)
HBM = pl.BlockSpec(memory_space=pltpu.HBM)


def dot(a, b):
    return jnp.dot(a, b, preferred_element_type=F32)


def onehot(shape, rows_to_cols):
    r = lax.broadcasted_iota(jnp.int32, shape, 0)
    c = lax.broadcasted_iota(jnp.int32, shape, 1)
    return jnp.where(rows_to_cols(r, c), 1.0, 0.0).astype(BF16)


def attention_kernel(
    n_chunks, sub_ref, len_hbm, q_hbm, nk_hbm, nv_hbm, res_hbm, k_hbm, v_hbm, wo_hbm,
    out_ref, len_ref, q_ref, nk_ref, nv_ref, res_ref, kbuf, vbuf, wobuf, sc_ref, w_ref, mix_ref,
    ho_ref, ssem, ksem, vsem, wsem,
):
    rows, heads, hd = q_ref.shape
    win = kbuf.shape[1]
    per = rows // n_chunks
    scale = 1.0 / math.sqrt(hd)
    half = wobuf.shape[0] // 2
    kcp = [
        pltpu.make_async_copy(k_hbm.at[pl.ds(c * per, per), 0], kbuf.at[pl.ds(c * per, per)], ksem.at[c])
        for c in range(n_chunks)
    ]
    vcp = [
        pltpu.make_async_copy(v_hbm.at[pl.ds(c * per, per), 0], vbuf.at[pl.ds(c * per, per)], vsem.at[c])
        for c in range(n_chunks)
    ]
    wcp = [
        pltpu.make_async_copy(wo_hbm.at[pl.ds(c * half, half)], wobuf.at[pl.ds(c * half, half)], wsem.at[c])
        for c in range(2)
    ]
    small = [
        pltpu.make_async_copy(src, dst, ssem.at[i])
        for i, (src, dst) in enumerate(
            ((q_hbm, q_ref), (len_hbm, len_ref), (nk_hbm, nk_ref), (nv_hbm, nv_ref), (res_hbm, res_ref))
        )
    ]
    for cp in small + kcp + vcp + wcp:
        cp.start()
    for cp in small:
        cp.wait()

    q = q_ref[...].astype(F32)
    own = jnp.sum(q * nk_ref[...].astype(F32)[:, None, :], -1, keepdims=True) * scale
    new_v = nv_ref[...].astype(F32)
    slot = lax.broadcasted_iota(jnp.int32, (heads, win), 1)
    for c in range(n_chunks):
        kcp[c].wait()
        for b in range(c * per, (c + 1) * per):
            s = lax.dot_general(q_ref[b], kbuf[b], (((1,), (1,)), ((), ())), preferred_element_type=F32)
            sc_ref[b] = jnp.where(slot < len_ref[b], s * scale, -1e30)
    for c in range(n_chunks):
        r = pl.ds(c * per, per)
        sc = sc_ref[r]
        own_c = own[c * per : (c + 1) * per]
        top = jnp.maximum(jnp.max(sc, -1, keepdims=True), own_c)
        w = jnp.exp(sc - top)
        ow = jnp.exp(own_c - top)
        den = jnp.sum(w, -1, keepdims=True) + ow
        w_ref[r] = w.astype(BF16)
        owv = ow.astype(BF16).astype(F32) * new_v[c * per : (c + 1) * per, None, :]
        vcp[c].wait()
        for b in range(c * per, (c + 1) * per):
            i = b - c * per
            mix_ref[pl.ds(b * heads, heads)] = (dot(w_ref[b], vbuf[b]) + owv[i]) / den[i]

    dev_rows = rows // 2
    tail = dev_rows - SUBL
    order = [(0, SUBL), (dev_rows, SUBL), (SUBL, tail), (dev_rows + SUBL, tail)]
    for h in range(heads):
        at = 0
        for first, n in order:
            piece = mix_ref[pl.ds(first * heads + h, n, stride=heads), :]
            ho_ref[pl.ds(at, n), pl.ds(h * hd, hd)] = piece
            at += n
    ho = ho_ref[...].astype(BF16)
    wcp[0].wait()
    acc = dot(ho[:, :half], wobuf[:half])
    wcp[1].wait()
    out_ref[...] = acc + dot(ho[:, half:], wobuf[half:])
    sub = sub_ref[0]
    res = res_ref[...].astype(F32)

    @pl.when(sub == 0)
    def _():
        out_ref[pl.ds(0, SUBL)] += res[:SUBL]
        out_ref[pl.ds(2 * SUBL, tail)] += res[SUBL:]

    @pl.when(sub == 1)
    def _():
        out_ref[pl.ds(SUBL, SUBL)] += res[:SUBL]
        out_ref[pl.ds(2 * SUBL + tail, tail)] += res[SUBL:]


def norm_kernel(experts, sub_ref, a_ref, b_ref, gain_ref, route_ref, rw_ref, pay_ref, stream_ref, nrm_ref):
    rows, width = a_ref.shape
    dev_rows = rows // 2
    tail = dev_rows - SUBL
    cols = width // 2
    chunks = 2 * SUBL // (2 * tail)
    cw = cols // chunks
    s0 = sub_ref[0] == 0
    stream = a_ref[...] + b_ref[...]
    mean = jnp.mean(stream * stream, -1, keepdims=True)
    normed = stream * lax.rsqrt(mean + 1e-06) * gain_ref[...]
    nrm_ref[...] = jnp.where(s0, normed[:, :cols], normed[:, cols:])
    main = nrm_ref[pl.ds(0, 2 * SUBL)]
    rest = nrm_ref[pl.ds(2 * SUBL, 2 * tail)]
    folded = jnp.concatenate([rest[:, c * cw : (c + 1) * cw] for c in range(chunks)], 0)
    pay_ref[:, pl.ds(0, cols)] = main.astype(BF16)
    pay_ref[:, pl.ds(cols, cw)] = folded.astype(BF16)
    stream_ref[pl.ds(0, SUBL)] = jnp.where(s0, stream[:SUBL], stream[SUBL : 2 * SUBL])
    stream_ref[pl.ds(SUBL, tail)] = jnp.where(
        s0, stream[2 * SUBL : 2 * SUBL + tail], stream[2 * SUBL + tail :]
    )
    lane = lax.broadcasted_iota(jnp.int32, (dev_rows, 2 * experts), 1)
    which = jnp.where(lane < experts, lane, lane - experts)
    route, rw = route_ref[...], rw_ref[...]
    dense = jnp.zeros((dev_rows, 2 * experts), F32)
    for k in range(route.shape[1]):
        dense += jnp.where(route[:, k : k + 1] == which, rw[:, k : k + 1], 0.0)
    high = dense.astype(BF16).astype(F32)
    pair = jnp.where(lane < experts, high, dense - high)
    pad = jnp.zeros((SUBL - tail, 2 * experts), F32)
    first = jnp.concatenate([pair[:SUBL], pair[SUBL:], pad], 0)
    second = jnp.concatenate([pair[SUBL:], pad, pair[:SUBL]], 0)
    pay_ref[:, pl.ds(cols + cw, 2 * experts)] = jnp.where(s0, first, second).astype(BF16)


def unpack_tokens(x_ref, piece_ref, cols, chunks):
    blocks, br, _ = piece_ref.shape
    tail = br // chunks
    cw = cols // chunks
    x_ref[pl.ds(0, blocks * br)] = piece_ref[:, :, pl.ds(0, cols)].reshape(blocks * br, cols)
    folded = piece_ref[:, :, pl.ds(cols, cw)].reshape(blocks * br, cw)
    for c in range(chunks):
        pick = onehot(
            (blocks * tail, blocks * br),
            lambda r, q: q == (r // tail) * br + c * tail + r % tail,
        )
        x_ref[pl.ds(blocks * br, blocks * tail), pl.ds(c * cw, cw)] = dot(pick, folded).astype(BF16)


def load_kernel(n_src, spans, *refs):
    srcs, outs, sem = refs[:n_src], refs[n_src + 1 : -1], refs[-1]
    copies = [
        pltpu.make_async_copy(srcs[i].at[pl.ds(first, n)], outs[j], sem.at[j])
        for j, (i, first, n) in enumerate(spans)
    ]
    for cp in copies:
        cp.start()
    for cp in copies:
        cp.wait()


def first_half_kernel(
    chunks, sub_ref, piece_ref, ga_ref, gb_ref, ua_ref, up_hbm, g_ref, u_ref, ub_ref, x_ref, sem
):
    n, width, _ = ga_ref.shape
    cols = width // 2
    rest = [pltpu.make_async_copy(up_hbm.at[n + e], ub_ref.at[e], sem.at[e]) for e in range(n)]
    for cp in rest:
        cp.start()
    unpack_tokens(x_ref, piece_ref, cols, chunks)
    at = pl.ds(pl.multiple_of(sub_ref[0] * cols, cols), cols)
    for e in range(n):
        g_ref[e] = dot(x_ref[...], ga_ref[e, at, :])
        u_ref[e] = dot(x_ref[...], ua_ref[e, at, :])
        g_ref[n + e] = dot(x_ref[...], gb_ref[e, at, :])
    for e in range(n):
        rest[e].wait()
        u_ref[n + e] = dot(x_ref[...], ub_ref[e, at, :])


def second_half_kernel(
    chunks, sub_ref, ep_ref, own_ref, oth_ref, g_ref, u_ref, ga_ref, gb_ref, ua_ref, ub_ref, down_hbm,
    keep_ref, send_ref, x_ref, acc_ref, comb_ref, hid_ref, down_ref, sem,
):
    n, _, width = down_ref.shape
    downs = [pltpu.make_async_copy(down_hbm.at[e], down_ref.at[e], sem.at[e]) for e in range(n)]
    for cp in downs:
        cp.start()
    cols = width // 2
    blocks, br, wide = oth_ref.shape
    cw = cols // chunks
    experts = (wide - cols - cw) // 2
    tail = br // chunks
    sub = sub_ref[0]
    s0 = sub == 0
    unpack_tokens(x_ref, oth_ref, cols, chunks)
    at = pl.ds(pl.multiple_of((1 - sub) * cols, cols), cols)

    mine = own_ref[:, :, pl.ds(cols + cw, 2 * experts)]
    other = oth_ref[:, :, pl.ds(cols + cw, 2 * experts)]
    c0 = jnp.where(s0, mine, other)
    c1 = jnp.where(s0, other, mine)
    row = lax.broadcasted_iota(jnp.int32, c0.shape, 1)
    comb_ref[pl.ds(0, blocks * br)] = (
        jnp.where(row < SUBL, c0, c1).astype(F32).reshape(blocks * br, 2 * experts)
    )
    ht = tail // 2
    shape = (blocks * tail, blocks * br)
    pick0 = onehot(shape, lambda r, q: (r % tail < ht) & (q == (r // tail) * br + SUBL + r % tail))
    pick1 = onehot(shape, lambda r, q: (r % tail >= ht) & (q == (r // tail) * br + r % tail - ht))
    comb_ref[pl.ds(blocks * br, blocks * tail)] = dot(
        pick0, c0.reshape(blocks * br, 2 * experts)
    ) + dot(pick1, c1.reshape(blocks * br, 2 * experts))
    lane = lax.broadcasted_iota(jnp.int32, comb_ref.shape, 1)
    first_expert = (2 * ep_ref[0] + sub) * n
    comb = comb_ref[...]
    part = n // 2
    for e in range(n):
        gate_ref, up_ref, i = (ga_ref, ua_ref, e) if e < part else (gb_ref, ub_ref, e - part)
        gate = g_ref[e] + dot(x_ref[...], gate_ref[i, at, :])
        up = u_ref[e] + dot(x_ref[...], up_ref[i, at, :])
        hid_ref[e] = (gate / (1.0 + jnp.exp(-gate)) * up).astype(BF16)
    for e in range(n):
        mine_e = (lane == first_expert + e) | (lane == first_expert + e + experts)
        weight = jnp.sum(jnp.where(mine_e, comb, 0.0), -1, keepdims=True)
        downs[e].wait()
        y = dot(hid_ref[e], down_ref[e]).astype(BF16).astype(F32) * weight
        acc_ref[...] = y if e == 0 else acc_ref[...] + y

    ow = width // (SUBL // ht)
    main = acc_ref[pl.ds(0, blocks * br)].reshape(blocks, 2, SUBL, width)
    m0, m1 = main[:, 0], main[:, 1]
    keep_ref[:, :, pl.ds(0, width)] = jnp.where(s0, m0, m1)
    send_ref[:, :, pl.ds(0, width)] = jnp.where(s0, m1, m0).astype(BF16)
    rest = acc_ref[pl.ds(blocks * br, blocks * tail)].astype(BF16)
    for ref, side in ((keep_ref, sub), (send_ref, 1 - sub)):
        total = jnp.zeros((blocks * SUBL, ow), F32)
        for c in range(SUBL // ht):
            pick = onehot(
                (blocks * SUBL, blocks * tail),
                lambda r, q: ((r % SUBL) // ht == c) & (q == (r // SUBL) * tail + ht * side + r % ht),
            )
            total += dot(pick, rest[:, c * ow : (c + 1) * ow])
        ref[:, :, pl.ds(width, ow)] = total.reshape(blocks, SUBL, ow).astype(ref.dtype)


def finish_kernel(stream_ref, a_ref, b_ref, out_ref):
    dev_rows, width = stream_ref.shape
    tail = dev_rows - SUBL
    chunks = SUBL // tail
    ow = width // chunks
    total = a_ref[...] + b_ref[...].astype(F32)
    out_ref[pl.ds(0, SUBL)] = (stream_ref[pl.ds(0, SUBL)] + total[:, :width]).astype(BF16)
    rest = jnp.concatenate([total[c * tail : (c + 1) * tail, width:] for c in range(chunks)], 1)
    out_ref[pl.ds(SUBL, tail)] = (stream_ref[pl.ds(SUBL, tail)] + rest).astype(BF16)


def params(mib):
    return pltpu.CompilerParams(vmem_limit_bytes=mib << 20)


def per_device(
    queries, cache_keys, cache_values, new_keys, new_values, lengths, out_proj, residual,
    norm_gain, gate_proj, up_proj, down_proj, routing, route_weights,
):
    queries, cache_keys, cache_values, lengths, out_proj, residual, gate_proj, up_proj, down_proj = (
        pltpu.with_memory_space_constraint(x, pltpu.HBM)
        for x in (
            queries, cache_keys, cache_values, lengths, out_proj, residual, gate_proj, up_proj, down_proj
        )
    )
    rows, heads, hd = queries.shape
    win = cache_keys.shape[2]
    width = residual.shape[1]
    dev_rows = residual.shape[0]
    n_ep = lax.axis_size("ep")
    n_exp = gate_proj.shape[0]
    ff = gate_proj.shape[2]
    experts = n_exp * n_ep * lax.axis_size("sub")
    tail = dev_rows - SUBL
    cols = width // 2
    chunks = SUBL // tail
    cw = cols // chunks
    br = 2 * SUBL
    n_chunks = 4
    tokens = n_ep * rows
    sub = lax.axis_index("sub").astype(jnp.int32).reshape(1)
    ep = lax.axis_index("ep").astype(jnp.int32).reshape(1)
    swap = [(0, 1), (1, 0)]

    def to(x, m):
        return lax.ppermute(x, "ep", [(i, i ^ m) for i in range(n_ep)])

    partial = pl.pallas_call(
        functools.partial(attention_kernel, n_chunks),
        in_specs=[SMEM] + [HBM] * 8,
        out_specs=VMEM,
        out_shape=jax.ShapeDtypeStruct((rows, width), F32),
        scratch_shapes=[
            pltpu.SMEM((rows,), jnp.int32),
            pltpu.VMEM(queries.shape, BF16),
            pltpu.VMEM((rows, hd), BF16),
            pltpu.VMEM((rows, hd), BF16),
            pltpu.VMEM(residual.shape, BF16),
            pltpu.VMEM((rows, win, hd), BF16),
            pltpu.VMEM((rows, win, hd), BF16),
            pltpu.VMEM(out_proj.shape, BF16),
            pltpu.VMEM((rows, heads, win), F32),
            pltpu.VMEM((rows, heads, win), BF16),
            pltpu.VMEM((rows * heads, hd), F32),
            pltpu.VMEM((rows, heads * hd), F32),
            pltpu.SemaphoreType.DMA((5,)),
            pltpu.SemaphoreType.DMA((n_chunks,)),
            pltpu.SemaphoreType.DMA((n_chunks,)),
            pltpu.SemaphoreType.DMA((2,)),
        ],
        compiler_params=params(14),
        name="attention",
    )(
        sub, lengths, queries, new_keys.reshape(rows, hd), new_values.reshape(rows, hd), residual,
        cache_keys, cache_values, out_proj,
    )

    from_sibling = lax.ppermute(partial, "sub", swap)
    payload, stream = pl.pallas_call(
        functools.partial(norm_kernel, experts),
        in_specs=[SMEM] + [VMEM] * 5,
        out_specs=(VMEM, VMEM),
        out_shape=(
            jax.ShapeDtypeStruct((br, cols + cw + 2 * experts), BF16),
            jax.ShapeDtypeStruct((dev_rows, width), F32),
        ),
        scratch_shapes=[pltpu.VMEM((rows, cols), F32)],
        compiler_params=params(6),
        name="norm",
    )(sub, partial, from_sibling, norm_gain.reshape(1, width), routing, route_weights)

    part = n_exp // 2
    part_shape = pltpu.VMEM((part, width, ff), BF16)

    def load(srcs, spans, after, name):
        return pl.pallas_call(
            functools.partial(load_kernel, len(srcs), spans),
            in_specs=[HBM] * (len(srcs) + 1),
            out_specs=(VMEM,) * len(spans),
            out_shape=(part_shape,) * len(spans),
            scratch_shapes=[pltpu.SemaphoreType.DMA((len(spans),))],
            compiler_params=params(1),
            cost_estimate=pl.CostEstimate(
                flops=0, transcendentals=0, bytes_accessed=len(spans) * part * width * ff * 2
            ),
            name=name,
        )(*srcs, after)

    pieces = payload[None]
    far = []
    m = n_ep // 2
    while m >= 4:
        far.append(m)
        pieces = jnp.concatenate([pieces, to(pieces, m)], 0)
        m //= 2
    near = list(range(1, min(4, n_ep)))
    (gate_a,) = load((gate_proj,), ((0, 0, part),), payload, "load_first")
    gate_b, up_a = load((gate_proj, up_proj), ((0, part, part), (1, 0, part)), pieces, "load_second")
    pieces = jnp.concatenate([pieces] + [to(pieces, m) for m in near], 0)
    others = lax.ppermute(pieces, "sub", swap)

    half_shape = jax.ShapeDtypeStruct((n_exp, tokens, ff), F32)
    gate_half, up_half, up_b = pl.pallas_call(
        functools.partial(first_half_kernel, chunks),
        in_specs=[SMEM, VMEM, VMEM, VMEM, VMEM, HBM],
        out_specs=(VMEM,) * 3,
        out_shape=(half_shape, half_shape, part_shape),
        scratch_shapes=[pltpu.VMEM((tokens, cols), BF16), pltpu.SemaphoreType.DMA((part,))],
        compiler_params=params(4),
        name="experts_first",
    )(sub, pieces, gate_a, gate_b, up_a, up_proj)

    ow = width // chunks
    keep, send = pl.pallas_call(
        functools.partial(second_half_kernel, chunks),
        in_specs=[SMEM, SMEM] + [VMEM] * 8 + [HBM],
        out_specs=(VMEM, VMEM),
        out_shape=(
            jax.ShapeDtypeStruct((n_ep, SUBL, width + ow), F32),
            jax.ShapeDtypeStruct((n_ep, SUBL, width + ow), BF16),
        ),
        scratch_shapes=[
            pltpu.VMEM((tokens, cols), BF16),
            pltpu.VMEM((tokens, width), F32),
            pltpu.VMEM((tokens, 2 * experts), F32),
            pltpu.VMEM((n_exp, tokens, ff), BF16),
            pltpu.VMEM(down_proj.shape, BF16),
            pltpu.SemaphoreType.DMA((n_exp,)),
        ],
        compiler_params=params(20),
        name="experts_second",
    )(sub, ep, pieces, others, gate_half, up_half, gate_a, gate_b, up_a, up_b, down_proj)

    sums = keep + lax.ppermute(send, "sub", swap).astype(F32)
    size = n_ep // (len(near) + 1)
    arrived = [to(sums[i * size : (i + 1) * size].astype(BF16), m) for i, m in enumerate(near, 1)]
    sums = sums[:size]
    for x in arrived:
        sums = sums + x.astype(F32)
    last = None
    for m in reversed(far):
        size //= 2
        if last is not None:
            sums = sums + last.astype(F32)
        last = to(sums[size:].astype(BF16), m)
        sums = sums[:size]
    if last is None:
        last = jnp.zeros(sums.shape, BF16)

    return pl.pallas_call(
        finish_kernel,
        in_specs=[VMEM] * 3,
        out_specs=VMEM,
        out_shape=jax.ShapeDtypeStruct((dev_rows, width), BF16),
        compiler_params=params(4),
        name="finish",
    )(stream, sums[0], last[0])


def solution(mesh):
    return jax.shard_map(
        per_device,
        mesh=mesh,
        in_specs=(
            P(("grp", "ep"), "sub", None),
            P(("grp", "ep"), "sub", None, None),
            P(("grp", "ep"), "sub", None, None),
            P(("grp", "ep"), "sub", None),
            P(("grp", "ep"), "sub", None),
            P(("grp", "ep")),
            P("sub", None),
            P(("grp", "ep", "sub"), None),
            P(),
            P(("ep", "sub"), None, None),
            P(("ep", "sub"), None, None),
            P(("ep", "sub"), None, None),
            P(("grp", "ep", "sub"), None),
            P(("grp", "ep", "sub"), None),
        ),
        out_specs=P(("grp", "ep", "sub"), None),
        check_vma=False,
    )
```

```python
import functools
import math

import jax
import jax.numpy as jnp
from jax import lax
from jax.experimental import pallas as pl
from jax.experimental.pallas import tpu as pltpu
from jax.sharding import PartitionSpec as P


F32 = jnp.float32
BF16 = jnp.bfloat16
SUBL = 8

VMEM = pl.BlockSpec(memory_space=pltpu.VMEM)
SMEM = pl.BlockSpec(memory_space=pltpu.SMEM)
HBM = pl.BlockSpec(memory_space=pltpu.HBM)


def dot(a, b):
    return jnp.dot(a, b, preferred_element_type=F32)


def onehot(shape, rows_to_cols):
    r = lax.broadcasted_iota(jnp.int32, shape, 0)
    c = lax.broadcasted_iota(jnp.int32, shape, 1)
    return jnp.where(rows_to_cols(r, c), 1.0, 0.0).astype(BF16)


def attention_kernel(
    n_chunks, place_ref, len_hbm, q_hbm, nk_hbm, nv_hbm, res_hbm, k_hbm, v_hbm, wo_hbm,
    out_ref, len_ref, q_ref, nk_ref, nv_ref, res_ref, kbuf, vbuf, wobuf, sc_ref, w_ref, mix_ref,
    ho_ref, ssem, ksem, vsem, wsem,
):
    rows, heads, hd = q_ref.shape
    win = kbuf.shape[1]
    per = rows // n_chunks
    scale = 1.0 / math.sqrt(hd)
    half = wobuf.shape[0] // 2
    kcp = [
        pltpu.make_async_copy(k_hbm.at[pl.ds(c * per, per), 0], kbuf.at[pl.ds(c * per, per)], ksem.at[c])
        for c in range(n_chunks)
    ]
    vcp = [
        pltpu.make_async_copy(v_hbm.at[pl.ds(c * per, per), 0], vbuf.at[pl.ds(c * per, per)], vsem.at[c])
        for c in range(n_chunks)
    ]
    wcp = [
        pltpu.make_async_copy(wo_hbm.at[pl.ds(c * half, half)], wobuf.at[pl.ds(c * half, half)], wsem.at[c])
        for c in range(2)
    ]
    small = [
        pltpu.make_async_copy(src, dst, ssem.at[i])
        for i, (src, dst) in enumerate(
            ((q_hbm, q_ref), (len_hbm, len_ref), (nk_hbm, nk_ref), (nv_hbm, nv_ref), (res_hbm, res_ref))
        )
    ]
    for cp in small + kcp + vcp + wcp:
        cp.start()
    for cp in small:
        cp.wait()

    q = q_ref[...].astype(F32)
    own = jnp.sum(q * nk_ref[...].astype(F32)[:, None, :], -1, keepdims=True) * scale
    new_v = nv_ref[...].astype(F32)
    slot = lax.broadcasted_iota(jnp.int32, (heads, win), 1)
    for c in range(n_chunks):
        kcp[c].wait()
        for b in range(c * per, (c + 1) * per):
            s = lax.dot_general(q_ref[b], kbuf[b], (((1,), (1,)), ((), ())), preferred_element_type=F32)
            sc_ref[b] = jnp.where(slot < len_ref[b], s * scale, -1e30)
    for c in range(n_chunks):
        r = pl.ds(c * per, per)
        sc = sc_ref[r]
        own_c = own[c * per : (c + 1) * per]
        top = jnp.maximum(jnp.max(sc, -1, keepdims=True), own_c)
        w = jnp.exp(sc - top)
        ow = jnp.exp(own_c - top)
        den = jnp.sum(w, -1, keepdims=True) + ow
        w_ref[r] = w.astype(BF16)
        owv = ow.astype(BF16).astype(F32) * new_v[c * per : (c + 1) * per, None, :]
        vcp[c].wait()
        for b in range(c * per, (c + 1) * per):
            i = b - c * per
            mix_ref[pl.ds(b * heads, heads)] = (dot(w_ref[b], vbuf[b]) + owv[i]) / den[i]

    dev_rows = rows // 2
    tail = dev_rows - SUBL
    order = [(0, SUBL), (dev_rows, SUBL), (SUBL, tail), (dev_rows + SUBL, tail)]
    for h in range(heads):
        at = 0
        for first, n in order:
            piece = mix_ref[pl.ds(first * heads + h, n, stride=heads), :]
            ho_ref[pl.ds(at, n), pl.ds(h * hd, hd)] = piece
            at += n
    ho = ho_ref[...].astype(BF16)
    wcp[0].wait()
    acc = dot(ho[:, :half], wobuf[:half])
    wcp[1].wait()
    out_ref[...] = acc + dot(ho[:, half:], wobuf[half:])
    sub = place_ref[0]
    res = res_ref[...].astype(F32)

    @pl.when(sub == 0)
    def _():
        out_ref[pl.ds(0, SUBL)] += res[:SUBL]
        out_ref[pl.ds(2 * SUBL, tail)] += res[SUBL:]

    @pl.when(sub == 1)
    def _():
        out_ref[pl.ds(SUBL, SUBL)] += res[:SUBL]
        out_ref[pl.ds(2 * SUBL + tail, tail)] += res[SUBL:]


def norm_kernel(experts, place_ref, a_ref, b_ref, gain_ref, route_ref, rw_ref, pay_ref, stream_ref, nrm_ref):
    rows, width = a_ref.shape
    dev_rows = rows // 2
    tail = dev_rows - SUBL
    cols = width // 2
    chunks = 2 * SUBL // (2 * tail)
    cw = cols // chunks
    s0 = place_ref[0] == 0
    stream = a_ref[...] + b_ref[...]
    mean = jnp.mean(stream * stream, -1, keepdims=True)
    normed = stream * lax.rsqrt(mean + 1e-06) * gain_ref[...]
    nrm_ref[...] = jnp.where(s0, normed[:, :cols], normed[:, cols:])
    main = nrm_ref[pl.ds(0, 2 * SUBL)]
    rest = nrm_ref[pl.ds(2 * SUBL, 2 * tail)]
    folded = jnp.concatenate([rest[:, c * cw : (c + 1) * cw] for c in range(chunks)], 0)
    pay_ref[:, pl.ds(0, cols)] = main.astype(BF16)
    pay_ref[:, pl.ds(cols, cw)] = folded.astype(BF16)
    stream_ref[pl.ds(0, SUBL)] = jnp.where(s0, stream[:SUBL], stream[SUBL : 2 * SUBL])
    stream_ref[pl.ds(SUBL, tail)] = jnp.where(
        s0, stream[2 * SUBL : 2 * SUBL + tail], stream[2 * SUBL + tail :]
    )
    lane = lax.broadcasted_iota(jnp.int32, (dev_rows, 2 * experts), 1)
    which = jnp.where(lane < experts, lane, lane - experts)
    route, rw = route_ref[...], rw_ref[...]
    dense = jnp.zeros((dev_rows, 2 * experts), F32)
    for k in range(route.shape[1]):
        dense += jnp.where(route[:, k : k + 1] == which, rw[:, k : k + 1], 0.0)
    high = dense.astype(BF16).astype(F32)
    pair = jnp.where(lane < experts, high, dense - high)
    pad = jnp.zeros((SUBL - tail, 2 * experts), F32)
    first = jnp.concatenate([pair[:SUBL], pair[SUBL:], pad], 0)
    second = jnp.concatenate([pair[SUBL:], pad, pair[:SUBL]], 0)
    pay_ref[:, pl.ds(cols + cw, 2 * experts)] = jnp.where(s0, first, second).astype(BF16)


def unpack_tokens(x_ref, piece_ref, cols, chunks):
    blocks, br, _ = piece_ref.shape
    tail = br // chunks
    cw = cols // chunks
    x_ref[pl.ds(0, blocks * br)] = piece_ref[:, :, pl.ds(0, cols)].reshape(blocks * br, cols)
    folded = piece_ref[:, :, pl.ds(cols, cw)].reshape(blocks * br, cw)
    for c in range(chunks):
        pick = onehot(
            (blocks * tail, blocks * br),
            lambda r, q: q == (r // tail) * br + c * tail + r % tail,
        )
        x_ref[pl.ds(blocks * br, blocks * tail), pl.ds(c * cw, cw)] = dot(pick, folded).astype(BF16)


def load_kernel(n_src, spans, *refs):
    srcs, outs, sem = refs[:n_src], refs[n_src + 1 : -1], refs[-1]
    copies = [
        pltpu.make_async_copy(srcs[i].at[pl.ds(first, n)], outs[j], sem.at[j])
        for j, (i, first, n) in enumerate(spans)
    ]
    for cp in copies:
        cp.start()
    for cp in copies:
        cp.wait()


def first_half_kernel(
    chunks, place_ref, piece_ref, ga_ref, gb_ref, ua_ref, up_hbm, g_ref, u_ref, ub_ref, x_ref, sem
):
    n, width, _ = ga_ref.shape
    cols = width // 2
    rest = [pltpu.make_async_copy(up_hbm.at[n + e], ub_ref.at[e], sem.at[e]) for e in range(n)]
    for cp in rest:
        cp.start()
    unpack_tokens(x_ref, piece_ref, cols, chunks)
    at = pl.ds(pl.multiple_of(place_ref[0] * cols, cols), cols)
    for e in range(n):
        g_ref[e] = dot(x_ref[...], ga_ref[e, at, :])
        u_ref[e] = dot(x_ref[...], ua_ref[e, at, :])
        g_ref[n + e] = dot(x_ref[...], gb_ref[e, at, :])
    for e in range(n):
        rest[e].wait()
        u_ref[n + e] = dot(x_ref[...], ub_ref[e, at, :])


def second_half_kernel(
    chunks, place_ref, own_ref, oth_ref, g_ref, u_ref, ga_ref, gb_ref, ua_ref, ub_ref, down_hbm,
    keep_ref, send_ref, x_ref, acc_ref, comb_ref, hid_ref, down_ref, sem,
):
    n, _, width = down_ref.shape
    downs = [pltpu.make_async_copy(down_hbm.at[e], down_ref.at[e], sem.at[e]) for e in range(n)]
    for cp in downs:
        cp.start()
    cols = width // 2
    blocks, br, wide = oth_ref.shape
    cw = cols // chunks
    experts = (wide - cols - cw) // 2
    tail = br // chunks
    sub = place_ref[0]
    s0 = sub == 0
    unpack_tokens(x_ref, oth_ref, cols, chunks)
    at = pl.ds(pl.multiple_of((1 - sub) * cols, cols), cols)

    mine = own_ref[:, :, pl.ds(cols + cw, 2 * experts)]
    other = oth_ref[:, :, pl.ds(cols + cw, 2 * experts)]
    c0 = jnp.where(s0, mine, other)
    c1 = jnp.where(s0, other, mine)
    row = lax.broadcasted_iota(jnp.int32, c0.shape, 1)
    comb_ref[pl.ds(0, blocks * br)] = (
        jnp.where(row < SUBL, c0, c1).astype(F32).reshape(blocks * br, 2 * experts)
    )
    ht = tail // 2
    shape = (blocks * tail, blocks * br)
    pick0 = onehot(shape, lambda r, q: (r % tail < ht) & (q == (r // tail) * br + SUBL + r % tail))
    pick1 = onehot(shape, lambda r, q: (r % tail >= ht) & (q == (r // tail) * br + r % tail - ht))
    comb_ref[pl.ds(blocks * br, blocks * tail)] = dot(
        pick0, c0.reshape(blocks * br, 2 * experts)
    ) + dot(pick1, c1.reshape(blocks * br, 2 * experts))
    lane = lax.broadcasted_iota(jnp.int32, comb_ref.shape, 1)
    first_expert = (2 * place_ref[1] + sub) * n
    comb = comb_ref[...]
    part = n // 2
    for e in range(n):
        gate_ref, up_ref, i = (ga_ref, ua_ref, e) if e < part else (gb_ref, ub_ref, e - part)
        gate = g_ref[e] + dot(x_ref[...], gate_ref[i, at, :])
        up = u_ref[e] + dot(x_ref[...], up_ref[i, at, :])
        hid_ref[e] = (gate / (1.0 + jnp.exp(-gate)) * up).astype(BF16)
    for e in range(n):
        mine_e = (lane == first_expert + e) | (lane == first_expert + e + experts)
        weight = jnp.sum(jnp.where(mine_e, comb, 0.0), -1, keepdims=True)
        downs[e].wait()
        y = dot(hid_ref[e], down_ref[e]).astype(BF16).astype(F32) * weight
        acc_ref[...] = y if e == 0 else acc_ref[...] + y

    ow = width // (SUBL // ht)
    main = acc_ref[pl.ds(0, blocks * br)].reshape(blocks, 2, SUBL, width)
    m0, m1 = main[:, 0], main[:, 1]
    keep_ref[:, :, pl.ds(0, width)] = jnp.where(s0, m0, m1)
    send_ref[:, :, pl.ds(0, width)] = jnp.where(s0, m1, m0).astype(BF16)
    rest = acc_ref[pl.ds(blocks * br, blocks * tail)].astype(BF16)
    for ref, side in ((keep_ref, sub), (send_ref, 1 - sub)):
        total = jnp.zeros((blocks * SUBL, ow), F32)
        for c in range(SUBL // ht):
            pick = onehot(
                (blocks * SUBL, blocks * tail),
                lambda r, q: ((r % SUBL) // ht == c) & (q == (r // SUBL) * tail + ht * side + r % ht),
            )
            total += dot(pick, rest[:, c * ow : (c + 1) * ow])
        ref[:, :, pl.ds(width, ow)] = total.reshape(blocks, SUBL, ow).astype(ref.dtype)


def finish_kernel(stream_ref, a_ref, b_ref, out_ref):
    dev_rows, width = stream_ref.shape
    tail = dev_rows - SUBL
    chunks = SUBL // tail
    total = a_ref[...] + b_ref[...].astype(F32)
    out_ref[pl.ds(0, SUBL)] = (stream_ref[pl.ds(0, SUBL)] + total[:, :width]).astype(BF16)
    rest = jnp.concatenate([total[c * tail : (c + 1) * tail, width:] for c in range(chunks)], 1)
    out_ref[pl.ds(SUBL, tail)] = (stream_ref[pl.ds(SUBL, tail)] + rest).astype(BF16)


def params(mib):
    return pltpu.CompilerParams(vmem_limit_bytes=mib << 20)


def layer(
    queries, cache_keys, cache_values, new_keys, new_values, lengths, out_proj, residual,
    norm_gain, gate_proj, up_proj, down_proj, routing, route_weights,
):
    rows, heads, hd = queries.shape
    in_hbm = functools.partial(pltpu.with_memory_space_constraint, memory_space=pltpu.HBM)
    gate_proj, up_proj, down_proj = map(in_hbm, (gate_proj, up_proj, down_proj))
    win = cache_keys.shape[2]
    width = residual.shape[1]
    dev_rows = residual.shape[0]
    n_ep = lax.axis_size("ep")
    n_exp = gate_proj.shape[0]
    ff = gate_proj.shape[2]
    experts = n_exp * n_ep * lax.axis_size("sub")
    tail = dev_rows - SUBL
    cols = width // 2
    chunks = SUBL // tail
    cw = cols // chunks
    br = 2 * SUBL
    n_chunks = 4
    tokens = n_ep * rows
    place = jnp.stack([lax.axis_index("sub"), lax.axis_index("ep")]).astype(jnp.int32)
    swap = [(0, 1), (1, 0)]

    def to(x, m):
        return lax.ppermute(x, "ep", [(i, i ^ m) for i in range(n_ep)])

    partial = pl.pallas_call(
        functools.partial(attention_kernel, n_chunks),
        in_specs=[SMEM] + [HBM] * 8,
        out_specs=VMEM,
        out_shape=jax.ShapeDtypeStruct((rows, width), F32),
        scratch_shapes=[
            pltpu.SMEM((rows,), jnp.int32),
            pltpu.VMEM(queries.shape, BF16),
            pltpu.VMEM((rows, hd), BF16),
            pltpu.VMEM((rows, hd), BF16),
            pltpu.VMEM(residual.shape, BF16),
            pltpu.VMEM((rows, win, hd), BF16),
            pltpu.VMEM((rows, win, hd), BF16),
            pltpu.VMEM(out_proj.shape, BF16),
            pltpu.VMEM((rows, heads, win), F32),
            pltpu.VMEM((rows, heads, win), BF16),
            pltpu.VMEM((rows * heads, hd), F32),
            pltpu.VMEM((rows, heads * hd), F32),
            pltpu.SemaphoreType.DMA((5,)),
            pltpu.SemaphoreType.DMA((n_chunks,)),
            pltpu.SemaphoreType.DMA((n_chunks,)),
            pltpu.SemaphoreType.DMA((2,)),
        ],
        compiler_params=params(14),
        name="attention",
    )(
        place,
        *map(
            in_hbm,
            (
                lengths, queries, new_keys.reshape(rows, hd), new_values.reshape(rows, hd), residual,
                cache_keys, cache_values, out_proj,
            ),
        ),
    )

    from_sibling = lax.ppermute(partial, "sub", swap)
    payload, stream = pl.pallas_call(
        functools.partial(norm_kernel, experts),
        in_specs=[SMEM] + [VMEM] * 5,
        out_specs=(VMEM, VMEM),
        out_shape=(
            jax.ShapeDtypeStruct((br, cols + cw + 2 * experts), BF16),
            jax.ShapeDtypeStruct((dev_rows, width), F32),
        ),
        scratch_shapes=[pltpu.VMEM((rows, cols), F32)],
        compiler_params=params(6),
        name="norm",
    )(place, partial, from_sibling, norm_gain.reshape(1, width), routing, route_weights)

    part = n_exp // 2
    part_shape = pltpu.VMEM((part, width, ff), BF16)

    def load(srcs, spans, after):
        return pl.pallas_call(
            functools.partial(load_kernel, len(srcs), spans),
            in_specs=[HBM] * (len(srcs) + 1),
            out_specs=(VMEM,) * len(spans),
            out_shape=(part_shape,) * len(spans),
            scratch_shapes=[pltpu.SemaphoreType.DMA((len(spans),))],
            compiler_params=params(17),
        )(*srcs, after)

    pieces = payload[None]
    far = []
    m = n_ep // 2
    while m >= 4:
        far.append(m)
        got = to(pieces, m)
        pieces = jnp.concatenate([pieces, got], 0)
        m //= 2
    near = list(range(1, min(4, n_ep)))
    (gate_a,) = load((gate_proj,), ((0, 0, part),), payload)
    gate_b, up_a = load((gate_proj, up_proj), ((0, part, part), (1, 0, part)), pieces)
    got = []
    for m in near:
        got.append(to(pieces, m))
    pieces = jnp.concatenate([pieces] + got, 0)
    others = lax.ppermute(pieces, "sub", swap)

    half_shape = jax.ShapeDtypeStruct((n_exp, tokens, ff), F32)
    gate_half, up_half, up_b = pl.pallas_call(
        functools.partial(first_half_kernel, chunks),
        in_specs=[SMEM, VMEM, VMEM, VMEM, VMEM, HBM],
        out_specs=(VMEM,) * 3,
        out_shape=(half_shape, half_shape, part_shape),
        scratch_shapes=[pltpu.VMEM((tokens, cols), BF16), pltpu.SemaphoreType.DMA((part,))],
        compiler_params=params(17),
        name="experts_first",
    )(place, pieces, gate_a, gate_b, up_a, up_proj)

    ow = width // chunks
    keep, send = pl.pallas_call(
        functools.partial(second_half_kernel, chunks),
        in_specs=[SMEM] + [VMEM] * 8 + [HBM],
        out_specs=(VMEM, VMEM),
        out_shape=(
            jax.ShapeDtypeStruct((n_ep, SUBL, width + ow), F32),
            jax.ShapeDtypeStruct((n_ep, SUBL, width + ow), BF16),
        ),
        scratch_shapes=[
            pltpu.VMEM((tokens, cols), BF16),
            pltpu.VMEM((tokens, width), F32),
            pltpu.VMEM((tokens, 2 * experts), F32),
            pltpu.VMEM((n_exp, tokens, ff), BF16),
            pltpu.VMEM(down_proj.shape, BF16),
            pltpu.SemaphoreType.DMA((n_exp,)),
        ],
        compiler_params=params(17),
        name="experts_second",
    )(place, pieces, others, gate_half, up_half, gate_a, gate_b, up_a, up_b, down_proj)

    sums = keep + lax.ppermute(send, "sub", swap).astype(F32)
    size = n_ep // (len(near) + 1)
    arrived = [to(sums[i * size : (i + 1) * size].astype(BF16), m) for i, m in enumerate(near, 1)]
    sums = sums[:size]
    for x in arrived:
        sums = sums + x.astype(F32)
    last = None
    for m in reversed(far):
        size //= 2
        if last is not None:
            sums = sums + last.astype(F32)
        last = to(sums[size:].astype(BF16), m)
        sums = sums[:size]
    if last is None:
        last = jnp.zeros(sums.shape, BF16)

    return pl.pallas_call(
        finish_kernel,
        in_specs=[VMEM] * 3,
        out_specs=VMEM,
        out_shape=jax.ShapeDtypeStruct((dev_rows, width), BF16),
        compiler_params=params(4),
        name="finish",
    )(stream, sums[0], last[0])


def solution(mesh):
    return build(mesh)


def build(mesh):
    return jax.shard_map(
        layer,
        mesh=mesh,
        in_specs=(
            P(("grp", "ep"), "sub", None),
            P(("grp", "ep"), "sub", None, None),
            P(("grp", "ep"), "sub", None, None),
            P(("grp", "ep"), "sub", None),
            P(("grp", "ep"), "sub", None),
            P(("grp", "ep")),
            P("sub", None),
            P(("grp", "ep", "sub"), None),
            P(),
            P(("ep", "sub"), None, None),
            P(("ep", "sub"), None, None),
            P(("ep", "sub"), None, None),
            P(("grp", "ep", "sub"), None),
            P(("grp", "ep", "sub"), None),
        ),
        out_specs=P(("grp", "ep", "sub"), None),
        check_vma=False,
    )
```

```python
import functools
import math

import jax
import jax.numpy as jnp
from jax import lax
from jax.experimental import pallas as pl
from jax.experimental.pallas import tpu as pltpu
from jax.sharding import PartitionSpec as P


F32 = jnp.float32
BF16 = jnp.bfloat16
SUBL = 8

VMEM = pl.BlockSpec(memory_space=pltpu.VMEM)
SMEM = pl.BlockSpec(memory_space=pltpu.SMEM)
HBM = pl.BlockSpec(memory_space=pltpu.HBM)


def dot(a, b):
    return jnp.dot(a, b, preferred_element_type=F32)


def onehot(shape, rows_to_cols):
    r = lax.broadcasted_iota(jnp.int32, shape, 0)
    c = lax.broadcasted_iota(jnp.int32, shape, 1)
    return jnp.where(rows_to_cols(r, c), 1.0, 0.0).astype(BF16)


def attention_kernel(
    n_chunks, len_hbm, q_hbm, nk_hbm, nv_hbm, res_hbm, k_hbm, v_hbm, wo_hbm,
    out_ref, len_ref, q_ref, nk_ref, nv_ref, res_ref, kbuf, vbuf, wobuf, sc_ref, w_ref, mix_ref,
    ho_ref, ssem, ksem, vsem, wsem,
):
    rows, heads, hd = q_ref.shape
    win = kbuf.shape[1]
    per = rows // n_chunks
    scale = 1.0 / math.sqrt(hd)
    half = wobuf.shape[0] // 2
    kcp = [
        pltpu.make_async_copy(k_hbm.at[pl.ds(c * per, per), 0], kbuf.at[pl.ds(c * per, per)], ksem.at[c])
        for c in range(n_chunks)
    ]
    vcp = [
        pltpu.make_async_copy(v_hbm.at[pl.ds(c * per, per), 0], vbuf.at[pl.ds(c * per, per)], vsem.at[c])
        for c in range(n_chunks)
    ]
    wcp = [
        pltpu.make_async_copy(wo_hbm.at[pl.ds(c * half, half)], wobuf.at[pl.ds(c * half, half)], wsem.at[c])
        for c in range(2)
    ]
    small = [
        pltpu.make_async_copy(src, dst, ssem.at[i])
        for i, (src, dst) in enumerate(
            ((q_hbm, q_ref), (len_hbm, len_ref), (nk_hbm, nk_ref), (nv_hbm, nv_ref), (res_hbm, res_ref))
        )
    ]
    for cp in small + kcp + vcp + wcp:
        cp.start()
    for cp in small:
        cp.wait()

    q = q_ref[...].astype(F32)
    own = jnp.sum(q * nk_ref[...].astype(F32)[:, None, :], -1, keepdims=True) * scale
    new_v = nv_ref[...].astype(F32)
    slot = lax.broadcasted_iota(jnp.int32, (heads, win), 1)
    for c in range(n_chunks):
        kcp[c].wait()
        for b in range(c * per, (c + 1) * per):
            s = lax.dot_general(q_ref[b], kbuf[b], (((1,), (1,)), ((), ())), preferred_element_type=F32)
            sc_ref[b] = jnp.where(slot < len_ref[b], s * scale, -1e30)
    for c in range(n_chunks):
        r = pl.ds(c * per, per)
        sc = sc_ref[r]
        own_c = own[c * per : (c + 1) * per]
        top = jnp.maximum(jnp.max(sc, -1, keepdims=True), own_c)
        w = jnp.exp(sc - top)
        ow = jnp.exp(own_c - top)
        den = jnp.sum(w, -1, keepdims=True) + ow
        w_ref[r] = w.astype(BF16)
        owv = ow.astype(BF16).astype(F32) * new_v[c * per : (c + 1) * per, None, :]
        vcp[c].wait()
        for b in range(c * per, (c + 1) * per):
            i = b - c * per
            mix_ref[pl.ds(b * heads, heads)] = (dot(w_ref[b], vbuf[b]) + owv[i]) / den[i]

    dev_rows = rows // 2
    tail = dev_rows - SUBL
    order = [(0, SUBL), (dev_rows, SUBL), (SUBL, tail), (dev_rows + SUBL, tail)]
    for h in range(heads):
        at = 0
        for first, n in order:
            piece = mix_ref[pl.ds(first * heads + h, n, stride=heads), :]
            ho_ref[pl.ds(at, n), pl.ds(h * hd, hd)] = piece
            at += n
    ho = ho_ref[...].astype(BF16)
    wcp[0].wait()
    acc = dot(ho[:, :half], wobuf[:half])
    wcp[1].wait()
    out_ref[...] = acc + dot(ho[:, half:], wobuf[half:])
    sub = lax.axis_index("sub")
    res = res_ref[...].astype(F32)

    @pl.when(sub == 0)
    def _():
        out_ref[pl.ds(0, SUBL)] += res[:SUBL]
        out_ref[pl.ds(2 * SUBL, tail)] += res[SUBL:]

    @pl.when(sub == 1)
    def _():
        out_ref[pl.ds(SUBL, SUBL)] += res[:SUBL]
        out_ref[pl.ds(2 * SUBL + tail, tail)] += res[SUBL:]


def norm_kernel(experts, a_ref, b_ref, gain_ref, route_ref, rw_ref, _g, _u, _d, pay_ref, stream_ref, nrm_ref):
    rows, width = a_ref.shape
    dev_rows = rows // 2
    tail = dev_rows - SUBL
    cols = width // 2
    chunks = 2 * SUBL // (2 * tail)
    cw = cols // chunks
    s0 = lax.axis_index("sub") == 0
    stream = a_ref[...] + b_ref[...]
    mean = jnp.mean(stream * stream, -1, keepdims=True)
    normed = stream * lax.rsqrt(mean + 1e-06) * gain_ref[...]
    nrm_ref[...] = jnp.where(s0, normed[:, :cols], normed[:, cols:])
    main = nrm_ref[pl.ds(0, 2 * SUBL)]
    rest = nrm_ref[pl.ds(2 * SUBL, 2 * tail)]
    folded = jnp.concatenate([rest[:, c * cw : (c + 1) * cw] for c in range(chunks)], 0)
    pay_ref[:, pl.ds(0, cols)] = main.astype(BF16)
    pay_ref[:, pl.ds(cols, cw)] = folded.astype(BF16)
    stream_ref[pl.ds(0, SUBL)] = jnp.where(s0, stream[:SUBL], stream[SUBL : 2 * SUBL])
    stream_ref[pl.ds(SUBL, tail)] = jnp.where(
        s0, stream[2 * SUBL : 2 * SUBL + tail], stream[2 * SUBL + tail :]
    )
    lane = lax.broadcasted_iota(jnp.int32, (dev_rows, 2 * experts), 1)
    which = jnp.where(lane < experts, lane, lane - experts)
    route, rw = route_ref[...], rw_ref[...]
    dense = jnp.zeros((dev_rows, 2 * experts), F32)
    for k in range(route.shape[1]):
        dense += jnp.where(route[:, k : k + 1] == which, rw[:, k : k + 1], 0.0)
    high = dense.astype(BF16).astype(F32)
    pair = jnp.where(lane < experts, high, dense - high)
    pad = jnp.zeros((SUBL - tail, 2 * experts), F32)
    first = jnp.concatenate([pair[:SUBL], pair[SUBL:], pad], 0)
    second = jnp.concatenate([pair[SUBL:], pad, pair[:SUBL]], 0)
    pay_ref[:, pl.ds(cols + cw, 2 * experts)] = jnp.where(s0, first, second).astype(BF16)


def join_kernel(*refs):
    out_ref, at = refs[-1], 0
    for ref in refs[:-1]:
        n = ref.shape[0]
        out_ref[pl.ds(at, n)] = ref[...]
        at += n


def join(arrays):
    rows = sum(x.shape[0] for x in arrays)
    return pl.pallas_call(
        join_kernel,
        in_specs=[VMEM] * len(arrays),
        out_specs=VMEM,
        out_shape=jax.ShapeDtypeStruct((rows,) + arrays[0].shape[1:], arrays[0].dtype),
        compiler_params=params(4),
    )(*arrays)


def unpack_tokens(x_ref, piece_ref, cols, chunks):
    blocks, br, _ = piece_ref.shape
    tail = br // chunks
    cw = cols // chunks
    x_ref[pl.ds(0, blocks * br)] = piece_ref[:, :, pl.ds(0, cols)].reshape(blocks * br, cols)
    folded = piece_ref[:, :, pl.ds(cols, cw)].reshape(blocks * br, cw)
    for c in range(chunks):
        pick = onehot(
            (blocks * tail, blocks * br),
            lambda r, q: q == (r // tail) * br + c * tail + r % tail,
        )
        x_ref[pl.ds(blocks * br, blocks * tail), pl.ds(c * cw, cw)] = dot(pick, folded).astype(BF16)


def first_half_kernel(chunks, piece_ref, gate_ref, up_ref, g_ref, u_ref, x_ref):
    n, width, _ = gate_ref.shape
    cols = width // 2
    unpack_tokens(x_ref, piece_ref, cols, chunks)
    at = pl.ds(pl.multiple_of(lax.axis_index("sub") * cols, cols), cols)
    for e in range(n):
        g_ref[e] = dot(x_ref[...], gate_ref[e, at, :])
        u_ref[e] = dot(x_ref[...], up_ref[e, at, :])


def second_half_kernel(chunks, oth_ref, g_ref, u_ref, gate_ref, up_ref, hid_ref, x_ref):
    n, width, _ = gate_ref.shape
    cols = width // 2
    unpack_tokens(x_ref, oth_ref, cols, chunks)
    at = pl.ds(pl.multiple_of((1 - lax.axis_index("sub")) * cols, cols), cols)
    for e in range(n):
        gate = g_ref[e] + dot(x_ref[...], gate_ref[e, at, :])
        up = u_ref[e] + dot(x_ref[...], up_ref[e, at, :])
        hid_ref[e] = (gate / (1.0 + jnp.exp(-gate)) * up).astype(BF16)


def third_kernel(chunks, own_ref, oth_ref, hid_ref, down_ref, keep_ref, send_ref, acc_ref, comb_ref):
    n, _, width = down_ref.shape
    cols = width // 2
    blocks, br, wide = oth_ref.shape
    cw = cols // chunks
    experts = (wide - cols - cw) // 2
    tail = br // chunks
    sub = lax.axis_index("sub")
    s0 = sub == 0
    mine = own_ref[:, :, pl.ds(cols + cw, 2 * experts)]
    other = oth_ref[:, :, pl.ds(cols + cw, 2 * experts)]
    c0 = jnp.where(s0, mine, other)
    c1 = jnp.where(s0, other, mine)
    row = lax.broadcasted_iota(jnp.int32, c0.shape, 1)
    comb_ref[pl.ds(0, blocks * br)] = (
        jnp.where(row < SUBL, c0, c1).astype(F32).reshape(blocks * br, 2 * experts)
    )
    ht = tail // 2
    shape = (blocks * tail, blocks * br)
    pick0 = onehot(shape, lambda r, q: (r % tail < ht) & (q == (r // tail) * br + SUBL + r % tail))
    pick1 = onehot(shape, lambda r, q: (r % tail >= ht) & (q == (r // tail) * br + r % tail - ht))
    comb_ref[pl.ds(blocks * br, blocks * tail)] = dot(
        pick0, c0.reshape(blocks * br, 2 * experts)
    ) + dot(pick1, c1.reshape(blocks * br, 2 * experts))
    lane = lax.broadcasted_iota(jnp.int32, comb_ref.shape, 1)
    first_expert = (2 * lax.axis_index("ep") + sub) * n
    comb = comb_ref[...]
    for e in range(n):
        mine_e = (lane == first_expert + e) | (lane == first_expert + e + experts)
        weight = jnp.sum(jnp.where(mine_e, comb, 0.0), -1, keepdims=True)
        y = dot(hid_ref[e], down_ref[e]).astype(BF16).astype(F32) * weight
        acc_ref[...] = y if e == 0 else acc_ref[...] + y

    ow = width // (SUBL // ht)
    main = acc_ref[pl.ds(0, blocks * br)].reshape(blocks, 2, SUBL, width)
    m0, m1 = main[:, 0], main[:, 1]
    keep_ref[:, :, pl.ds(0, width)] = jnp.where(s0, m0, m1)
    send_ref[:, :, pl.ds(0, width)] = jnp.where(s0, m1, m0).astype(BF16)
    rest = acc_ref[pl.ds(blocks * br, blocks * tail)].astype(BF16)
    for ref, side in ((keep_ref, sub), (send_ref, 1 - sub)):
        total = jnp.zeros((blocks * SUBL, ow), F32)
        for c in range(SUBL // ht):
            pick = onehot(
                (blocks * SUBL, blocks * tail),
                lambda r, q: ((r % SUBL) // ht == c) & (q == (r // SUBL) * tail + ht * side + r % ht),
            )
            total += dot(pick, rest[:, c * ow : (c + 1) * ow])
        ref[:, :, pl.ds(width, ow)] = total.reshape(blocks, SUBL, ow).astype(ref.dtype)


def finish_kernel(stream_ref, a_ref, b_ref, out_ref):
    dev_rows, width = stream_ref.shape
    tail = dev_rows - SUBL
    chunks = SUBL // tail
    total = a_ref[...] + b_ref[...].astype(F32)
    out_ref[pl.ds(0, SUBL)] = (stream_ref[pl.ds(0, SUBL)] + total[:, :width]).astype(BF16)
    rest = jnp.concatenate([total[c * tail : (c + 1) * tail, width:] for c in range(chunks)], 1)
    out_ref[pl.ds(SUBL, tail)] = (stream_ref[pl.ds(SUBL, tail)] + rest).astype(BF16)


def params(mib):
    return pltpu.CompilerParams(vmem_limit_bytes=mib << 20)


def layer(
    queries, cache_keys, cache_values, new_keys, new_values, lengths, out_proj, residual,
    norm_gain, gate_proj, up_proj, down_proj, routing, route_weights,
):
    rows, heads, hd = queries.shape
    in_hbm = functools.partial(pltpu.with_memory_space_constraint, memory_space=pltpu.HBM)
    raw = (gate_proj, up_proj, down_proj)
    in_vmem = functools.partial(pltpu.with_memory_space_constraint, memory_space=pltpu.VMEM)
    gate_proj, up_proj, down_proj = map(in_vmem, (gate_proj, up_proj, down_proj))
    win = cache_keys.shape[2]
    width = residual.shape[1]
    dev_rows = residual.shape[0]
    n_ep = lax.axis_size("ep")
    n_exp = gate_proj.shape[0]
    ff = gate_proj.shape[2]
    experts = n_exp * n_ep * lax.axis_size("sub")
    tail = dev_rows - SUBL
    cols = width // 2
    chunks = SUBL // tail
    cw = cols // chunks
    br = 2 * SUBL
    n_chunks = 2
    tokens = n_ep * rows
    swap = [(0, 1), (1, 0)]

    def to(x, m):
        return lax.ppermute(x, "ep", [(i, i ^ m) for i in range(n_ep)])

    partial = pl.pallas_call(
        functools.partial(attention_kernel, n_chunks),
        in_specs=[HBM] * 8,
        out_specs=VMEM,
        out_shape=jax.ShapeDtypeStruct((rows, width), F32),
        scratch_shapes=[
            pltpu.SMEM((rows,), jnp.int32),
            pltpu.VMEM(queries.shape, BF16),
            pltpu.VMEM((rows, hd), BF16),
            pltpu.VMEM((rows, hd), BF16),
            pltpu.VMEM(residual.shape, BF16),
            pltpu.VMEM((rows, win, hd), BF16),
            pltpu.VMEM((rows, win, hd), BF16),
            pltpu.VMEM(out_proj.shape, BF16),
            pltpu.VMEM((rows, heads, win), F32),
            pltpu.VMEM((rows, heads, win), BF16),
            pltpu.VMEM((rows * heads, hd), F32),
            pltpu.VMEM((rows, heads * hd), F32),
            pltpu.SemaphoreType.DMA((5,)),
            pltpu.SemaphoreType.DMA((n_chunks,)),
            pltpu.SemaphoreType.DMA((n_chunks,)),
            pltpu.SemaphoreType.DMA((2,)),
        ],
        compiler_params=params(14),
        name="attention",
    )(
        *map(
            in_hbm,
            (
                lengths, queries, new_keys.reshape(rows, hd), new_values.reshape(rows, hd), residual,
                cache_keys, cache_values, out_proj,
            ),
        ),
    )

    from_sibling = lax.ppermute(partial, "sub", swap)
    payload, stream = pl.pallas_call(
        functools.partial(norm_kernel, experts),
        in_specs=[VMEM] * 5 + [HBM] * 3,
        out_specs=(VMEM, VMEM),
        out_shape=(
            jax.ShapeDtypeStruct((br, cols + cw + 2 * experts), BF16),
            jax.ShapeDtypeStruct((dev_rows, width), F32),
        ),
        scratch_shapes=[pltpu.VMEM((rows, cols), F32)],
        compiler_params=params(4),
        name="norm",
    )(partial, from_sibling, norm_gain.reshape(1, width), routing, route_weights, *map(in_hbm, raw))

    pieces = payload[None]
    far = []
    m = n_ep // 2
    while m >= 4:
        far.append(m)
        got = to(pieces, m)
        pieces = join([pieces, got])
        m //= 2
    near = list(range(1, min(4, n_ep)))
    got = []
    for m in near:
        got.append(to(pieces, m))
    pieces = join([pieces] + got)
    others = lax.ppermute(pieces, "sub", swap)

    half_shape = jax.ShapeDtypeStruct((n_exp, tokens, ff), F32)
    gate_half, up_half = pl.pallas_call(
        functools.partial(first_half_kernel, chunks),
        in_specs=[VMEM] * 3,
        out_specs=(VMEM,) * 2,
        out_shape=(half_shape, half_shape),
        scratch_shapes=[pltpu.VMEM((tokens, cols), BF16)],
        compiler_params=params(4),
        name="experts_first",
    )(pieces, gate_proj, up_proj)

    hidden = pl.pallas_call(
        functools.partial(second_half_kernel, chunks),
        in_specs=[VMEM] * 5,
        out_specs=VMEM,
        out_shape=jax.ShapeDtypeStruct((n_exp, tokens, ff), BF16),
        scratch_shapes=[pltpu.VMEM((tokens, cols), BF16)],
        compiler_params=params(4),
        name="experts_second",
    )(others, gate_half, up_half, gate_proj, up_proj)

    ow = width // chunks
    keep, send = pl.pallas_call(
        functools.partial(third_kernel, chunks),
        in_specs=[VMEM] * 4,
        out_specs=(VMEM, VMEM),
        out_shape=(
            jax.ShapeDtypeStruct((n_ep, SUBL, width + ow), F32),
            jax.ShapeDtypeStruct((n_ep, SUBL, width + ow), BF16),
        ),
        scratch_shapes=[pltpu.VMEM((tokens, width), F32), pltpu.VMEM((tokens, 2 * experts), F32)],
        compiler_params=params(4),
        name="experts_third",
    )(pieces, others, hidden, down_proj)

    sums = keep + lax.ppermute(send, "sub", swap).astype(F32)
    size = n_ep // (len(near) + 1)
    arrived = [to(sums[i * size : (i + 1) * size].astype(BF16), m) for i, m in enumerate(near, 1)]
    sums = sums[:size]
    for x in arrived:
        sums = sums + x.astype(F32)
    last = None
    for m in reversed(far):
        size //= 2
        if last is not None:
            sums = sums + last.astype(F32)
        last = to(sums[size:].astype(BF16), m)
        sums = sums[:size]
    if last is None:
        last = jnp.zeros(sums.shape, BF16)

    return pl.pallas_call(
        finish_kernel,
        in_specs=[VMEM] * 3,
        out_specs=VMEM,
        out_shape=jax.ShapeDtypeStruct((dev_rows, width), BF16),
        compiler_params=params(4),
        name="finish",
    )(stream, sums[0], last[0])


def solution(mesh):
    return build(mesh)


def build(mesh):
    return jax.shard_map(
        layer,
        mesh=mesh,
        in_specs=(
            P(("grp", "ep"), "sub", None),
            P(("grp", "ep"), "sub", None, None),
            P(("grp", "ep"), "sub", None, None),
            P(("grp", "ep"), "sub", None),
            P(("grp", "ep"), "sub", None),
            P(("grp", "ep")),
            P("sub", None),
            P(("grp", "ep", "sub"), None),
            P(),
            P(("ep", "sub"), None, None),
            P(("ep", "sub"), None, None),
            P(("ep", "sub"), None, None),
            P(("grp", "ep", "sub"), None),
            P(("grp", "ep", "sub"), None),
        ),
        out_specs=P(("grp", "ep", "sub"), None),
        check_vma=False,
    )
```

```python
import functools
import math

import jax
import jax.numpy as jnp
from jax import lax
from jax.experimental import pallas as pl
from jax.experimental.pallas import tpu as pltpu
from jax.sharding import PartitionSpec as P


K_PARTS, V_PARTS, W_PARTS = 2, 1, 1
F32 = jnp.float32
BF16 = jnp.bfloat16
SUBL = 8

VMEM = pl.BlockSpec(memory_space=pltpu.VMEM)
SMEM = pl.BlockSpec(memory_space=pltpu.SMEM)
HBM = pl.BlockSpec(memory_space=pltpu.HBM)


def dot(a, b):
    return jnp.dot(a, b, preferred_element_type=F32)


def onehot(shape, rows_to_cols):
    r = lax.broadcasted_iota(jnp.int32, shape, 0)
    c = lax.broadcasted_iota(jnp.int32, shape, 1)
    return jnp.where(rows_to_cols(r, c), 1.0, 0.0).astype(BF16)


def attention_kernel(
    n_chunks, len_hbm, q_hbm, nk_hbm, nv_hbm, res_hbm, k_hbm, v_hbm, wo_hbm,
    out_ref, len_ref, q_ref, nk_ref, nv_ref, res_ref, kbuf, vbuf, wobuf, sc_ref, w_ref, mix_ref,
    ho_ref, ssem, ksem, vsem, wsem,
):
    rows, heads, hd = q_ref.shape
    win = kbuf.shape[1]
    per = rows // n_chunks
    scale = 1.0 / math.sqrt(hd)

    def split(src, dst, first, n, parts, sems):
        step = n // parts
        return [
            pltpu.make_async_copy(
                src.at[pl.ds(first + i * step, step)], dst.at[pl.ds(first + i * step, step)], sems.at[i]
            )
            for i in range(parts)
        ]

    kcp = [split(k_hbm.at[:, 0], kbuf, c * per, per, K_PARTS, ksem.at[c]) for c in range(n_chunks)]
    vcp = [split(v_hbm.at[:, 0], vbuf, c * per, per, V_PARTS, vsem.at[c]) for c in range(n_chunks)]
    n_w = W_PARTS
    step_w = wobuf.shape[0] // n_w
    wcp = split(wo_hbm, wobuf, 0, wobuf.shape[0], n_w, wsem)
    small = [
        pltpu.make_async_copy(src, dst, ssem.at[i])
        for i, (src, dst) in enumerate(
            ((q_hbm, q_ref), (len_hbm, len_ref), (nk_hbm, nk_ref), (nv_hbm, nv_ref), (res_hbm, res_ref))
        )
    ]
    for cp in small + sum(kcp, []) + sum(vcp, []) + wcp:
        cp.start()
    for cp in small:
        cp.wait()

    q = q_ref[...].astype(F32)
    own = jnp.sum(q * nk_ref[...].astype(F32)[:, None, :], -1, keepdims=True) * scale
    new_v = nv_ref[...].astype(F32)
    slot = lax.broadcasted_iota(jnp.int32, (heads, win), 1)
    for c in range(n_chunks):
        for cp in kcp[c]:
            cp.wait()
        for b in range(c * per, (c + 1) * per):
            s = lax.dot_general(q_ref[b], kbuf[b], (((1,), (1,)), ((), ())), preferred_element_type=F32)
            sc_ref[b] = jnp.where(slot < len_ref[b], s * scale, -1e30)
    for c in range(n_chunks):
        r = pl.ds(c * per, per)
        sc = sc_ref[r]
        own_c = own[c * per : (c + 1) * per]
        top = jnp.maximum(jnp.max(sc, -1, keepdims=True), own_c)
        w = jnp.exp(sc - top)
        ow = jnp.exp(own_c - top)
        den = jnp.sum(w, -1, keepdims=True) + ow
        w_ref[r] = w.astype(BF16)
        owv = ow.astype(BF16).astype(F32) * new_v[c * per : (c + 1) * per, None, :]
        for cp in vcp[c]:
            cp.wait()
        for b in range(c * per, (c + 1) * per):
            i = b - c * per
            mix_ref[pl.ds(b * heads, heads)] = (dot(w_ref[b], vbuf[b]) + owv[i]) / den[i]

    dev_rows = rows // 2
    tail = dev_rows - SUBL
    order = [(0, SUBL), (dev_rows, SUBL), (SUBL, tail), (dev_rows + SUBL, tail)]
    for h in range(heads):
        at = 0
        for first, n in order:
            piece = mix_ref[pl.ds(first * heads + h, n, stride=heads), :]
            ho_ref[pl.ds(at, n), pl.ds(h * hd, hd)] = piece
            at += n
    ho = ho_ref[...].astype(BF16)
    acc = None
    for i in range(n_w):
        wcp[i].wait()
        piece = dot(ho[:, i * step_w : (i + 1) * step_w], wobuf[pl.ds(i * step_w, step_w)])
        acc = piece if acc is None else acc + piece
    out_ref[...] = acc
    sub = lax.axis_index("sub")
    res = res_ref[...].astype(F32)

    @pl.when(sub == 0)
    def _():
        out_ref[pl.ds(0, SUBL)] += res[:SUBL]
        out_ref[pl.ds(2 * SUBL, tail)] += res[SUBL:]

    @pl.when(sub == 1)
    def _():
        out_ref[pl.ds(SUBL, SUBL)] += res[:SUBL]
        out_ref[pl.ds(2 * SUBL + tail, tail)] += res[SUBL:]


def norm_kernel(experts, a_ref, b_ref, gain_ref, route_ref, rw_ref, _g, _u, _d, pay_ref, stream_ref, nrm_ref):
    rows, width = a_ref.shape
    dev_rows = rows // 2
    tail = dev_rows - SUBL
    cols = width // 2
    chunks = 2 * SUBL // (2 * tail)
    cw = cols // chunks
    s0 = lax.axis_index("sub") == 0
    stream = a_ref[...] + b_ref[...]
    mean = jnp.mean(stream * stream, -1, keepdims=True)
    normed = stream * lax.rsqrt(mean + 1e-06) * gain_ref[...]
    nrm_ref[...] = jnp.where(s0, normed[:, :cols], normed[:, cols:])
    main = nrm_ref[pl.ds(0, 2 * SUBL)]
    rest = nrm_ref[pl.ds(2 * SUBL, 2 * tail)]
    folded = jnp.concatenate([rest[:, c * cw : (c + 1) * cw] for c in range(chunks)], 0)
    pay_ref[:, pl.ds(0, cols)] = main.astype(BF16)
    pay_ref[:, pl.ds(cols, cw)] = folded.astype(BF16)
    stream_ref[pl.ds(0, SUBL)] = jnp.where(s0, stream[:SUBL], stream[SUBL : 2 * SUBL])
    stream_ref[pl.ds(SUBL, tail)] = jnp.where(
        s0, stream[2 * SUBL : 2 * SUBL + tail], stream[2 * SUBL + tail :]
    )
    lane = lax.broadcasted_iota(jnp.int32, (dev_rows, 2 * experts), 1)
    which = jnp.where(lane < experts, lane, lane - experts)
    route, rw = route_ref[...], rw_ref[...]
    dense = jnp.zeros((dev_rows, 2 * experts), F32)
    for k in range(route.shape[1]):
        dense += jnp.where(route[:, k : k + 1] == which, rw[:, k : k + 1], 0.0)
    high = dense.astype(BF16).astype(F32)
    pair = jnp.where(lane < experts, high, dense - high)
    pad = jnp.zeros((SUBL - tail, 2 * experts), F32)
    first = jnp.concatenate([pair[:SUBL], pair[SUBL:], pad], 0)
    second = jnp.concatenate([pair[SUBL:], pad, pair[:SUBL]], 0)
    pay_ref[:, pl.ds(cols + cw, 2 * experts)] = jnp.where(s0, first, second).astype(BF16)


def join_kernel(*refs):
    out_ref, at = refs[-1], 0
    for ref in refs[:-1]:
        n = ref.shape[0]
        out_ref[pl.ds(at, n)] = ref[...]
        at += n


def join(arrays):
    rows = sum(x.shape[0] for x in arrays)
    return pl.pallas_call(
        join_kernel,
        in_specs=[VMEM] * len(arrays),
        out_specs=VMEM,
        out_shape=jax.ShapeDtypeStruct((rows,) + arrays[0].shape[1:], arrays[0].dtype),
        compiler_params=params(4),
    )(*arrays)


def unpack_tokens(x_ref, piece_ref, cols, chunks):
    blocks, br, _ = piece_ref.shape
    tail = br // chunks
    cw = cols // chunks
    x_ref[pl.ds(0, blocks * br)] = piece_ref[:, :, pl.ds(0, cols)].reshape(blocks * br, cols)
    folded = piece_ref[:, :, pl.ds(cols, cw)].reshape(blocks * br, cw)
    for c in range(chunks):
        pick = onehot(
            (blocks * tail, blocks * br),
            lambda r, q: q == (r // tail) * br + c * tail + r % tail,
        )
        x_ref[pl.ds(blocks * br, blocks * tail), pl.ds(c * cw, cw)] = dot(pick, folded).astype(BF16)


def first_half_kernel(chunks, piece_ref, gate_ref, up_ref, g_ref, u_ref, x_ref):
    n, width, _ = gate_ref.shape
    cols = width // 2
    unpack_tokens(x_ref, piece_ref, cols, chunks)
    at = pl.ds(pl.multiple_of(lax.axis_index("sub") * cols, cols), cols)
    for e in range(n):
        g_ref[e] = dot(x_ref[...], gate_ref[e, at, :])
        u_ref[e] = dot(x_ref[...], up_ref[e, at, :])


def second_half_kernel(chunks, oth_ref, g_ref, u_ref, gate_ref, up_ref, hid_ref, x_ref):
    n, width, _ = gate_ref.shape
    cols = width // 2
    unpack_tokens(x_ref, oth_ref, cols, chunks)
    at = pl.ds(pl.multiple_of((1 - lax.axis_index("sub")) * cols, cols), cols)
    for e in range(n):
        gate = g_ref[e] + dot(x_ref[...], gate_ref[e, at, :])
        up = u_ref[e] + dot(x_ref[...], up_ref[e, at, :])
        hid_ref[e] = (gate / (1.0 + jnp.exp(-gate)) * up).astype(BF16)


def third_kernel(chunks, own_ref, oth_ref, hid_ref, down_ref, keep_ref, send_ref, acc_ref, comb_ref):
    n, _, width = down_ref.shape
    cols = width // 2
    blocks, br, wide = oth_ref.shape
    cw = cols // chunks
    experts = (wide - cols - cw) // 2
    tail = br // chunks
    sub = lax.axis_index("sub")
    s0 = sub == 0
    mine = own_ref[:, :, pl.ds(cols + cw, 2 * experts)]
    other = oth_ref[:, :, pl.ds(cols + cw, 2 * experts)]
    c0 = jnp.where(s0, mine, other)
    c1 = jnp.where(s0, other, mine)
    row = lax.broadcasted_iota(jnp.int32, c0.shape, 1)
    comb_ref[pl.ds(0, blocks * br)] = (
        jnp.where(row < SUBL, c0, c1).astype(F32).reshape(blocks * br, 2 * experts)
    )
    ht = tail // 2
    shape = (blocks * tail, blocks * br)
    pick0 = onehot(shape, lambda r, q: (r % tail < ht) & (q == (r // tail) * br + SUBL + r % tail))
    pick1 = onehot(shape, lambda r, q: (r % tail >= ht) & (q == (r // tail) * br + r % tail - ht))
    comb_ref[pl.ds(blocks * br, blocks * tail)] = dot(
        pick0, c0.reshape(blocks * br, 2 * experts)
    ) + dot(pick1, c1.reshape(blocks * br, 2 * experts))
    lane = lax.broadcasted_iota(jnp.int32, comb_ref.shape, 1)
    first_expert = (2 * lax.axis_index("ep") + sub) * n
    comb = comb_ref[...]
    for e in range(n):
        mine_e = (lane == first_expert + e) | (lane == first_expert + e + experts)
        weight = jnp.sum(jnp.where(mine_e, comb, 0.0), -1, keepdims=True)
        y = dot(hid_ref[e], down_ref[e]).astype(BF16).astype(F32) * weight
        acc_ref[...] = y if e == 0 else acc_ref[...] + y

    ow = width // (SUBL // ht)
    main = acc_ref[pl.ds(0, blocks * br)].reshape(blocks, 2, SUBL, width)
    m0, m1 = main[:, 0], main[:, 1]
    keep_ref[:, :, pl.ds(0, width)] = jnp.where(s0, m0, m1)
    send_ref[:, :, pl.ds(0, width)] = jnp.where(s0, m1, m0).astype(BF16)
    rest = acc_ref[pl.ds(blocks * br, blocks * tail)].astype(BF16)
    for ref, side in ((keep_ref, sub), (send_ref, 1 - sub)):
        total = jnp.zeros((blocks * SUBL, ow), F32)
        for c in range(SUBL // ht):
            pick = onehot(
                (blocks * SUBL, blocks * tail),
                lambda r, q: ((r % SUBL) // ht == c) & (q == (r // SUBL) * tail + ht * side + r % ht),
            )
            total += dot(pick, rest[:, c * ow : (c + 1) * ow])
        ref[:, :, pl.ds(width, ow)] = total.reshape(blocks, SUBL, ow).astype(ref.dtype)


def finish_kernel(stream_ref, a_ref, b_ref, out_ref):
    dev_rows, width = stream_ref.shape
    tail = dev_rows - SUBL
    chunks = SUBL // tail
    total = a_ref[...] + b_ref[...].astype(F32)
    out_ref[pl.ds(0, SUBL)] = (stream_ref[pl.ds(0, SUBL)] + total[:, :width]).astype(BF16)
    rest = jnp.concatenate([total[c * tail : (c + 1) * tail, width:] for c in range(chunks)], 1)
    out_ref[pl.ds(SUBL, tail)] = (stream_ref[pl.ds(SUBL, tail)] + rest).astype(BF16)


def params(mib):
    return pltpu.CompilerParams(vmem_limit_bytes=mib << 20)


def layer(
    queries, cache_keys, cache_values, new_keys, new_values, lengths, out_proj, residual,
    norm_gain, gate_proj, up_proj, down_proj, routing, route_weights,
):
    rows, heads, hd = queries.shape
    in_hbm = functools.partial(pltpu.with_memory_space_constraint, memory_space=pltpu.HBM)
    raw = (gate_proj, up_proj, down_proj)
    in_vmem = functools.partial(pltpu.with_memory_space_constraint, memory_space=pltpu.VMEM)
    gate_proj, up_proj, down_proj = map(in_vmem, (gate_proj, up_proj, down_proj))
    win = cache_keys.shape[2]
    width = residual.shape[1]
    dev_rows = residual.shape[0]
    n_ep = lax.axis_size("ep")
    n_exp = gate_proj.shape[0]
    ff = gate_proj.shape[2]
    experts = n_exp * n_ep * lax.axis_size("sub")
    tail = dev_rows - SUBL
    cols = width // 2
    chunks = SUBL // tail
    cw = cols // chunks
    br = 2 * SUBL
    n_chunks = 2
    tokens = n_ep * rows
    swap = [(0, 1), (1, 0)]

    def to(x, m):
        return lax.ppermute(x, "ep", [(i, i ^ m) for i in range(n_ep)])

    partial = pl.pallas_call(
        functools.partial(attention_kernel, n_chunks),
        in_specs=[HBM] * 8,
        out_specs=VMEM,
        out_shape=jax.ShapeDtypeStruct((rows, width), F32),
        scratch_shapes=[
            pltpu.SMEM((rows,), jnp.int32),
            pltpu.VMEM(queries.shape, BF16),
            pltpu.VMEM((rows, hd), BF16),
            pltpu.VMEM((rows, hd), BF16),
            pltpu.VMEM(residual.shape, BF16),
            pltpu.VMEM((rows, win, hd), BF16),
            pltpu.VMEM((rows, win, hd), BF16),
            pltpu.VMEM(out_proj.shape, BF16),
            pltpu.VMEM((rows, heads, win), F32),
            pltpu.VMEM((rows, heads, win), BF16),
            pltpu.VMEM((rows * heads, hd), F32),
            pltpu.VMEM((rows, heads * hd), F32),
            pltpu.SemaphoreType.DMA((5,)),
            pltpu.SemaphoreType.DMA((n_chunks, K_PARTS)),
            pltpu.SemaphoreType.DMA((n_chunks, V_PARTS)),
            pltpu.SemaphoreType.DMA((W_PARTS,)),
        ],
        compiler_params=params(14),
        name="attention",
    )(
        *map(
            in_hbm,
            (
                lengths, queries, new_keys.reshape(rows, hd), new_values.reshape(rows, hd), residual,
                cache_keys, cache_values, out_proj,
            ),
        ),
    )

    from_sibling = lax.ppermute(partial, "sub", swap)
    payload, stream = pl.pallas_call(
        functools.partial(norm_kernel, experts),
        in_specs=[VMEM] * 5 + [HBM] * 3,
        out_specs=(VMEM, VMEM),
        out_shape=(
            jax.ShapeDtypeStruct((br, cols + cw + 2 * experts), BF16),
            jax.ShapeDtypeStruct((dev_rows, width), F32),
        ),
        scratch_shapes=[pltpu.VMEM((rows, cols), F32)],
        compiler_params=params(4),
        name="norm",
    )(partial, from_sibling, norm_gain.reshape(1, width), routing, route_weights, *map(in_hbm, raw))

    pieces = payload[None]
    far = []
    m = n_ep // 2
    while m >= 4:
        far.append(m)
        got = to(pieces, m)
        pieces = join([pieces, got])
        m //= 2
    near = list(range(1, min(4, n_ep)))
    got = []
    for m in near:
        got.append(to(pieces, m))
    pieces = join([pieces] + got)
    others = lax.ppermute(pieces, "sub", swap)

    half_shape = jax.ShapeDtypeStruct((n_exp, tokens, ff), F32)
    gate_half, up_half = pl.pallas_call(
        functools.partial(first_half_kernel, chunks),
        in_specs=[VMEM] * 3,
        out_specs=(VMEM,) * 2,
        out_shape=(half_shape, half_shape),
        scratch_shapes=[pltpu.VMEM((tokens, cols), BF16)],
        compiler_params=params(4),
        name="experts_first",
    )(pieces, gate_proj, up_proj)

    hidden = pl.pallas_call(
        functools.partial(second_half_kernel, chunks),
        in_specs=[VMEM] * 5,
        out_specs=VMEM,
        out_shape=jax.ShapeDtypeStruct((n_exp, tokens, ff), BF16),
        scratch_shapes=[pltpu.VMEM((tokens, cols), BF16)],
        compiler_params=params(4),
        name="experts_second",
    )(others, gate_half, up_half, gate_proj, up_proj)

    ow = width // chunks
    keep, send = pl.pallas_call(
        functools.partial(third_kernel, chunks),
        in_specs=[VMEM] * 4,
        out_specs=(VMEM, VMEM),
        out_shape=(
            jax.ShapeDtypeStruct((n_ep, SUBL, width + ow), F32),
            jax.ShapeDtypeStruct((n_ep, SUBL, width + ow), BF16),
        ),
        scratch_shapes=[pltpu.VMEM((tokens, width), F32), pltpu.VMEM((tokens, 2 * experts), F32)],
        compiler_params=params(4),
        name="experts_third",
    )(pieces, others, hidden, down_proj)

    sums = keep + lax.ppermute(send, "sub", swap).astype(F32)
    size = n_ep // (len(near) + 1)
    arrived = [to(sums[i * size : (i + 1) * size].astype(BF16), m) for i, m in enumerate(near, 1)]
    sums = sums[:size]
    for x in arrived:
        sums = sums + x.astype(F32)
    last = None
    for m in reversed(far):
        size //= 2
        if last is not None:
            sums = sums + last.astype(F32)
        last = to(sums[size:].astype(BF16), m)
        sums = sums[:size]
    if last is None:
        last = jnp.zeros(sums.shape, BF16)

    return pl.pallas_call(
        finish_kernel,
        in_specs=[VMEM] * 3,
        out_specs=VMEM,
        out_shape=jax.ShapeDtypeStruct((dev_rows, width), BF16),
        compiler_params=params(4),
        name="finish",
    )(stream, sums[0], last[0])


def solution(mesh):
    return build(mesh)


def build(mesh):
    return jax.shard_map(
        layer,
        mesh=mesh,
        in_specs=(
            P(("grp", "ep"), "sub", None),
            P(("grp", "ep"), "sub", None, None),
            P(("grp", "ep"), "sub", None, None),
            P(("grp", "ep"), "sub", None),
            P(("grp", "ep"), "sub", None),
            P(("grp", "ep")),
            P("sub", None),
            P(("grp", "ep", "sub"), None),
            P(),
            P(("ep", "sub"), None, None),
            P(("ep", "sub"), None, None),
            P(("ep", "sub"), None, None),
            P(("grp", "ep", "sub"), None),
            P(("grp", "ep", "sub"), None),
        ),
        out_specs=P(("grp", "ep", "sub"), None),
        check_vma=False,
    )
```

```python
import functools
import math

import jax
import jax.numpy as jnp
from jax import lax
from jax.experimental import pallas as pl
from jax.experimental.pallas import tpu as pltpu
from jax.sharding import PartitionSpec as P


K_PARTS, V_PARTS, W_PARTS = 2, 1, 1
F32 = jnp.float32
BF16 = jnp.bfloat16
SUBL = 8

VMEM = pl.BlockSpec(memory_space=pltpu.VMEM)
SMEM = pl.BlockSpec(memory_space=pltpu.SMEM)
HBM = pl.BlockSpec(memory_space=pltpu.HBM)


def dot(a, b):
    return jnp.dot(a, b, preferred_element_type=F32)


def onehot(shape, rows_to_cols):
    r = lax.broadcasted_iota(jnp.int32, shape, 0)
    c = lax.broadcasted_iota(jnp.int32, shape, 1)
    return jnp.where(rows_to_cols(r, c), 1.0, 0.0).astype(BF16)


def attention_kernel(
    n_chunks, len_hbm, q_hbm, nk_hbm, nv_hbm, res_hbm, k_hbm, v_hbm, wo_hbm,
    out_ref, len_ref, q_ref, nk_ref, nv_ref, res_ref, kbuf, vbuf, wobuf, sc_ref, w_ref, mix_ref,
    ho_ref, ssem, ksem, vsem, wsem,
):
    rows, heads, hd = q_ref.shape
    win = kbuf.shape[1]
    per = rows // n_chunks
    scale = 1.0 / math.sqrt(hd)

    def split(src, dst, first, n, parts, sems):
        step = n // parts
        return [
            pltpu.make_async_copy(
                src.at[pl.ds(first + i * step, step)], dst.at[pl.ds(first + i * step, step)], sems.at[i]
            )
            for i in range(parts)
        ]

    kcp = [split(k_hbm.at[:, 0], kbuf, c * per, per, K_PARTS, ksem.at[c]) for c in range(n_chunks)]
    vcp = [split(v_hbm.at[:, 0], vbuf, c * per, per, V_PARTS, vsem.at[c]) for c in range(n_chunks)]
    n_w = W_PARTS
    step_w = wobuf.shape[0] // n_w
    wcp = split(wo_hbm, wobuf, 0, wobuf.shape[0], n_w, wsem)
    small = [
        pltpu.make_async_copy(src, dst, ssem.at[i])
        for i, (src, dst) in enumerate(
            ((q_hbm, q_ref), (len_hbm, len_ref), (nk_hbm, nk_ref), (nv_hbm, nv_ref), (res_hbm, res_ref))
        )
    ]
    for cp in small + sum(kcp, []) + sum(vcp, []) + wcp:
        cp.start()
    for cp in small:
        cp.wait()

    q = q_ref[...].astype(F32)
    own = jnp.sum(q * nk_ref[...].astype(F32)[:, None, :], -1, keepdims=True) * scale
    new_v = nv_ref[...].astype(F32)
    slot = lax.broadcasted_iota(jnp.int32, (heads, win), 1)
    for c in range(n_chunks):
        for cp in kcp[c]:
            cp.wait()
        for b in range(c * per, (c + 1) * per):
            s = lax.dot_general(q_ref[b], kbuf[b], (((1,), (1,)), ((), ())), preferred_element_type=F32)
            sc_ref[b] = jnp.where(slot < len_ref[b], s * scale, -1e30)
    for c in range(n_chunks):
        r = pl.ds(c * per, per)
        sc = sc_ref[r]
        own_c = own[c * per : (c + 1) * per]
        top = jnp.maximum(jnp.max(sc, -1, keepdims=True), own_c)
        w = jnp.exp(sc - top)
        ow = jnp.exp(own_c - top)
        den = jnp.sum(w, -1, keepdims=True) + ow
        w_ref[r] = w.astype(BF16)
        owv = ow.astype(BF16).astype(F32) * new_v[c * per : (c + 1) * per, None, :]
        for cp in vcp[c]:
            cp.wait()
        for b in range(c * per, (c + 1) * per):
            i = b - c * per
            mix_ref[pl.ds(b * heads, heads)] = (dot(w_ref[b], vbuf[b]) + owv[i]) / den[i]

    dev_rows = rows // 2
    tail = dev_rows - SUBL
    order = [(0, SUBL), (dev_rows, SUBL), (SUBL, tail), (dev_rows + SUBL, tail)]
    for h in range(heads):
        at = 0
        for first, n in order:
            piece = mix_ref[pl.ds(first * heads + h, n, stride=heads), :]
            ho_ref[pl.ds(at, n), pl.ds(h * hd, hd)] = piece
            at += n
    ho = ho_ref[...].astype(BF16)
    acc = None
    for i in range(n_w):
        wcp[i].wait()
        piece = dot(ho[:, i * step_w : (i + 1) * step_w], wobuf[pl.ds(i * step_w, step_w)])
        acc = piece if acc is None else acc + piece
    out_ref[...] = acc
    sub = lax.axis_index("sub")
    res = res_ref[...].astype(F32)

    @pl.when(sub == 0)
    def _():
        out_ref[pl.ds(0, SUBL)] += res[:SUBL]
        out_ref[pl.ds(2 * SUBL, tail)] += res[SUBL:]

    @pl.when(sub == 1)
    def _():
        out_ref[pl.ds(SUBL, SUBL)] += res[:SUBL]
        out_ref[pl.ds(2 * SUBL + tail, tail)] += res[SUBL:]


def norm_kernel(experts, a_ref, b_ref, gain_ref, route_ref, rw_ref, _g, _u, _d, pay_ref, stream_ref, nrm_ref):
    rows, width = a_ref.shape
    dev_rows = rows // 2
    tail = dev_rows - SUBL
    cols = width // 2
    chunks = 2 * SUBL // (2 * tail)
    cw = cols // chunks
    s0 = lax.axis_index("sub") == 0
    stream = a_ref[...] + b_ref[...]
    mean = jnp.mean(stream * stream, -1, keepdims=True)
    normed = stream * lax.rsqrt(mean + 1e-06) * gain_ref[...]
    nrm_ref[...] = jnp.where(s0, normed[:, :cols], normed[:, cols:])
    main = nrm_ref[pl.ds(0, 2 * SUBL)]
    rest = nrm_ref[pl.ds(2 * SUBL, 2 * tail)]
    folded = jnp.concatenate([rest[:, c * cw : (c + 1) * cw] for c in range(chunks)], 0)
    pay_ref[:, pl.ds(0, cols)] = main.astype(BF16)
    pay_ref[:, pl.ds(cols, cw)] = folded.astype(BF16)
    stream_ref[pl.ds(0, SUBL)] = jnp.where(s0, stream[:SUBL], stream[SUBL : 2 * SUBL])
    stream_ref[pl.ds(SUBL, tail)] = jnp.where(
        s0, stream[2 * SUBL : 2 * SUBL + tail], stream[2 * SUBL + tail :]
    )
    lane = lax.broadcasted_iota(jnp.int32, (dev_rows, 2 * experts), 1)
    which = jnp.where(lane < experts, lane, lane - experts)
    route, rw = route_ref[...], rw_ref[...]
    dense = jnp.zeros((dev_rows, 2 * experts), F32)
    for k in range(route.shape[1]):
        dense += jnp.where(route[:, k : k + 1] == which, rw[:, k : k + 1], 0.0)
    high = dense.astype(BF16).astype(F32)
    pair = jnp.where(lane < experts, high, dense - high)
    pad = jnp.zeros((SUBL - tail, 2 * experts), F32)
    first = jnp.concatenate([pair[:SUBL], pair[SUBL:], pad], 0)
    second = jnp.concatenate([pair[SUBL:], pad, pair[:SUBL]], 0)
    pay_ref[:, pl.ds(cols + cw, 2 * experts)] = jnp.where(s0, first, second).astype(BF16)


def join_kernel(*refs):
    out_ref, at = refs[-1], 0
    for ref in refs[:-1]:
        n = ref.shape[0]
        out_ref[pl.ds(at, n)] = ref[...]
        at += n


def join(arrays):
    rows = sum(x.shape[0] for x in arrays)
    return pl.pallas_call(
        join_kernel,
        in_specs=[VMEM] * len(arrays),
        out_specs=VMEM,
        out_shape=jax.ShapeDtypeStruct((rows,) + arrays[0].shape[1:], arrays[0].dtype),
        compiler_params=params(4),
    )(*arrays)


def unpack_tokens(x_ref, piece_ref, cols, chunks, skip=0):
    br = piece_ref.shape[1]
    blocks = piece_ref.shape[0] - skip
    piece_ref = piece_ref.at[pl.ds(skip, blocks)]
    tail = br // chunks
    cw = cols // chunks
    x_ref[pl.ds(0, blocks * br)] = piece_ref[:, :, pl.ds(0, cols)].reshape(blocks * br, cols)
    folded = piece_ref[:, :, pl.ds(cols, cw)].reshape(blocks * br, cw)
    for c in range(chunks):
        pick = onehot(
            (blocks * tail, blocks * br),
            lambda r, q: q == (r // tail) * br + c * tail + r % tail,
        )
        x_ref[pl.ds(blocks * br, blocks * tail), pl.ds(c * cw, cw)] = dot(pick, folded).astype(BF16)


def first_half_kernel(chunks, skip, piece_ref, gate_ref, up_ref, g_ref, u_ref, x_ref):
    n, width, _ = gate_ref.shape
    cols = width // 2
    unpack_tokens(x_ref, piece_ref, cols, chunks, skip)
    at = pl.ds(pl.multiple_of(lax.axis_index("sub") * cols, cols), cols)
    for e in range(n):
        g_ref[e] = dot(x_ref[...], gate_ref[e, at, :])
        u_ref[e] = dot(x_ref[...], up_ref[e, at, :])


def second_half_kernel(
    chunks, oth_ref, ga_ref, ua_ref, gb_ref, ub_ref, gate_ref, up_ref, hid_ref, x_ref
):
    n, width, _ = gate_ref.shape
    cols = width // 2
    early = ga_ref.shape[1] * chunks // (chunks + 1)
    late = gb_ref.shape[1] * chunks // (chunks + 1)

    def whole(a, b):
        return jnp.concatenate([a[:early], b[:late], a[early:], b[late:]], 0)

    unpack_tokens(x_ref, oth_ref, cols, chunks)
    at = pl.ds(pl.multiple_of((1 - lax.axis_index("sub")) * cols, cols), cols)
    for e in range(n):
        gate = whole(ga_ref[e], gb_ref[e]) + dot(x_ref[...], gate_ref[e, at, :])
        up = whole(ua_ref[e], ub_ref[e]) + dot(x_ref[...], up_ref[e, at, :])
        hid_ref[e] = (gate / (1.0 + jnp.exp(-gate)) * up).astype(BF16)


def third_kernel(chunks, own_ref, oth_ref, hid_ref, down_ref, keep_ref, send_ref, acc_ref, comb_ref):
    n, _, width = down_ref.shape
    cols = width // 2
    blocks, br, wide = oth_ref.shape
    cw = cols // chunks
    experts = (wide - cols - cw) // 2
    tail = br // chunks
    sub = lax.axis_index("sub")
    s0 = sub == 0
    mine = own_ref[:, :, pl.ds(cols + cw, 2 * experts)]
    other = oth_ref[:, :, pl.ds(cols + cw, 2 * experts)]
    c0 = jnp.where(s0, mine, other)
    c1 = jnp.where(s0, other, mine)
    row = lax.broadcasted_iota(jnp.int32, c0.shape, 1)
    comb_ref[pl.ds(0, blocks * br)] = (
        jnp.where(row < SUBL, c0, c1).astype(F32).reshape(blocks * br, 2 * experts)
    )
    ht = tail // 2
    shape = (blocks * tail, blocks * br)
    pick0 = onehot(shape, lambda r, q: (r % tail < ht) & (q == (r // tail) * br + SUBL + r % tail))
    pick1 = onehot(shape, lambda r, q: (r % tail >= ht) & (q == (r // tail) * br + r % tail - ht))
    comb_ref[pl.ds(blocks * br, blocks * tail)] = dot(
        pick0, c0.reshape(blocks * br, 2 * experts)
    ) + dot(pick1, c1.reshape(blocks * br, 2 * experts))
    lane = lax.broadcasted_iota(jnp.int32, comb_ref.shape, 1)
    first_expert = (2 * lax.axis_index("ep") + sub) * n
    comb = comb_ref[...]
    for e in range(n):
        mine_e = (lane == first_expert + e) | (lane == first_expert + e + experts)
        weight = jnp.sum(jnp.where(mine_e, comb, 0.0), -1, keepdims=True)
        y = dot(hid_ref[e], down_ref[e]).astype(BF16).astype(F32) * weight
        acc_ref[...] = y if e == 0 else acc_ref[...] + y

    ow = width // (SUBL // ht)
    main = acc_ref[pl.ds(0, blocks * br)].reshape(blocks, 2, SUBL, width)
    m0, m1 = main[:, 0], main[:, 1]
    keep_ref[:, :, pl.ds(0, width)] = jnp.where(s0, m0, m1)
    send_ref[:, :, pl.ds(0, width)] = jnp.where(s0, m1, m0).astype(BF16)
    rest = acc_ref[pl.ds(blocks * br, blocks * tail)].astype(BF16)
    for ref, side in ((keep_ref, sub), (send_ref, 1 - sub)):
        total = jnp.zeros((blocks * SUBL, ow), F32)
        for c in range(SUBL // ht):
            pick = onehot(
                (blocks * SUBL, blocks * tail),
                lambda r, q: ((r % SUBL) // ht == c) & (q == (r // SUBL) * tail + ht * side + r % ht),
            )
            total += dot(pick, rest[:, c * ow : (c + 1) * ow])
        ref[:, :, pl.ds(width, ow)] = total.reshape(blocks, SUBL, ow).astype(ref.dtype)


def finish_kernel(stream_ref, a_ref, b_ref, out_ref):
    dev_rows, width = stream_ref.shape
    tail = dev_rows - SUBL
    chunks = SUBL // tail
    total = a_ref[...] + b_ref[...].astype(F32)
    out_ref[pl.ds(0, SUBL)] = (stream_ref[pl.ds(0, SUBL)] + total[:, :width]).astype(BF16)
    rest = jnp.concatenate([total[c * tail : (c + 1) * tail, width:] for c in range(chunks)], 1)
    out_ref[pl.ds(SUBL, tail)] = (stream_ref[pl.ds(SUBL, tail)] + rest).astype(BF16)


def params(mib):
    return pltpu.CompilerParams(vmem_limit_bytes=mib << 20)


def layer(
    queries, cache_keys, cache_values, new_keys, new_values, lengths, out_proj, residual,
    norm_gain, gate_proj, up_proj, down_proj, routing, route_weights,
):
    rows, heads, hd = queries.shape
    in_hbm = functools.partial(pltpu.with_memory_space_constraint, memory_space=pltpu.HBM)
    raw = (gate_proj, up_proj, down_proj)
    in_vmem = functools.partial(pltpu.with_memory_space_constraint, memory_space=pltpu.VMEM)
    gate_proj, up_proj, down_proj = map(in_vmem, (gate_proj, up_proj, down_proj))
    win = cache_keys.shape[2]
    width = residual.shape[1]
    dev_rows = residual.shape[0]
    n_ep = lax.axis_size("ep")
    n_exp = gate_proj.shape[0]
    ff = gate_proj.shape[2]
    experts = n_exp * n_ep * lax.axis_size("sub")
    tail = dev_rows - SUBL
    cols = width // 2
    chunks = SUBL // tail
    cw = cols // chunks
    br = 2 * SUBL
    n_chunks = 2
    tokens = n_ep * rows
    swap = [(0, 1), (1, 0)]

    def to(x, m):
        return lax.ppermute(x, "ep", [(i, i ^ m) for i in range(n_ep)])

    partial = pl.pallas_call(
        functools.partial(attention_kernel, n_chunks),
        in_specs=[HBM] * 8,
        out_specs=VMEM,
        out_shape=jax.ShapeDtypeStruct((rows, width), F32),
        scratch_shapes=[
            pltpu.SMEM((rows,), jnp.int32),
            pltpu.VMEM(queries.shape, BF16),
            pltpu.VMEM((rows, hd), BF16),
            pltpu.VMEM((rows, hd), BF16),
            pltpu.VMEM(residual.shape, BF16),
            pltpu.VMEM((rows, win, hd), BF16),
            pltpu.VMEM((rows, win, hd), BF16),
            pltpu.VMEM(out_proj.shape, BF16),
            pltpu.VMEM((rows, heads, win), F32),
            pltpu.VMEM((rows, heads, win), BF16),
            pltpu.VMEM((rows * heads, hd), F32),
            pltpu.VMEM((rows, heads * hd), F32),
            pltpu.SemaphoreType.DMA((5,)),
            pltpu.SemaphoreType.DMA((n_chunks, K_PARTS)),
            pltpu.SemaphoreType.DMA((n_chunks, V_PARTS)),
            pltpu.SemaphoreType.DMA((W_PARTS,)),
        ],
        compiler_params=params(14),
        name="attention",
    )(
        *map(
            in_hbm,
            (
                lengths, queries, new_keys.reshape(rows, hd), new_values.reshape(rows, hd), residual,
                cache_keys, cache_values, out_proj,
            ),
        ),
    )

    from_sibling = lax.ppermute(partial, "sub", swap)
    payload, stream = pl.pallas_call(
        functools.partial(norm_kernel, experts),
        in_specs=[VMEM] * 5 + [HBM] * 3,
        out_specs=(VMEM, VMEM),
        out_shape=(
            jax.ShapeDtypeStruct((br, cols + cw + 2 * experts), BF16),
            jax.ShapeDtypeStruct((dev_rows, width), F32),
        ),
        scratch_shapes=[pltpu.VMEM((rows, cols), F32)],
        compiler_params=params(4),
        name="norm",
    )(partial, from_sibling, norm_gain.reshape(1, width), routing, route_weights, *map(in_hbm, raw))

    pieces = payload[None]
    far = []
    m = n_ep // 2
    while m >= 4:
        far.append(m)
        got = to(pieces, m)
        pieces = join([pieces, got])
        m //= 2
    near = list(range(1, min(4, n_ep)))
    early = pieces
    got = []
    for m in near:
        got.append(to(pieces, m))
    pieces = join([pieces] + got)
    others = lax.ppermute(pieces, "sub", swap)

    def first_half(x, skip):
        n_rows = (x.shape[0] - skip) * rows
        shape = jax.ShapeDtypeStruct((n_exp, n_rows, ff), F32)
        return pl.pallas_call(
            functools.partial(first_half_kernel, chunks, skip),
            in_specs=[VMEM] * 3,
            out_specs=(VMEM,) * 2,
            out_shape=(shape, shape),
            scratch_shapes=[pltpu.VMEM((n_rows, cols), BF16)],
            compiler_params=params(4),
        )(x, gate_proj, up_proj)

    gate_early, up_early = first_half(early, 0)
    gate_late, up_late = first_half(pieces, early.shape[0])

    hidden = pl.pallas_call(
        functools.partial(second_half_kernel, chunks),
        in_specs=[VMEM] * 7,
        out_specs=VMEM,
        out_shape=jax.ShapeDtypeStruct((n_exp, tokens, ff), BF16),
        scratch_shapes=[pltpu.VMEM((tokens, cols), BF16)],
        compiler_params=params(4),
        name="experts_second",
    )(others, gate_early, up_early, gate_late, up_late, gate_proj, up_proj)

    ow = width // chunks
    keep, send = pl.pallas_call(
        functools.partial(third_kernel, chunks),
        in_specs=[VMEM] * 4,
        out_specs=(VMEM, VMEM),
        out_shape=(
            jax.ShapeDtypeStruct((n_ep, SUBL, width + ow), F32),
            jax.ShapeDtypeStruct((n_ep, SUBL, width + ow), BF16),
        ),
        scratch_shapes=[pltpu.VMEM((tokens, width), F32), pltpu.VMEM((tokens, 2 * experts), F32)],
        compiler_params=params(4),
        name="experts_third",
    )(pieces, others, hidden, down_proj)

    sums = keep + lax.ppermute(send, "sub", swap).astype(F32)
    size = n_ep // (len(near) + 1)
    arrived = []
    for i, m in enumerate(near, 1):
        arrived.append(to(sums[i * size : (i + 1) * size].astype(BF16), m))
    sums = sums[:size]
    for x in arrived:
        sums = sums + x.astype(F32)
    last = None
    for m in reversed(far):
        size //= 2
        if last is not None:
            sums = sums + last.astype(F32)
        last = to(sums[size:].astype(BF16), m)
        sums = sums[:size]
    if last is None:
        last = jnp.zeros(sums.shape, BF16)

    return pl.pallas_call(
        finish_kernel,
        in_specs=[VMEM] * 3,
        out_specs=VMEM,
        out_shape=jax.ShapeDtypeStruct((dev_rows, width), BF16),
        compiler_params=params(4),
        name="finish",
    )(stream, sums[0], last[0])


def solution(mesh):
    return build(mesh)


def build(mesh):
    return jax.shard_map(
        layer,
        mesh=mesh,
        in_specs=(
            P(("grp", "ep"), "sub", None),
            P(("grp", "ep"), "sub", None, None),
            P(("grp", "ep"), "sub", None, None),
            P(("grp", "ep"), "sub", None),
            P(("grp", "ep"), "sub", None),
            P(("grp", "ep")),
            P("sub", None),
            P(("grp", "ep", "sub"), None),
            P(),
            P(("ep", "sub"), None, None),
            P(("ep", "sub"), None, None),
            P(("ep", "sub"), None, None),
            P(("grp", "ep", "sub"), None),
            P(("grp", "ep", "sub"), None),
        ),
        out_specs=P(("grp", "ep", "sub"), None),
        check_vma=False,
    )
```

```python
import functools
import math

import jax
import jax.numpy as jnp
from jax import lax
from jax.experimental import pallas as pl
from jax.experimental.pallas import tpu as pltpu
from jax.sharding import PartitionSpec as P


K_PARTS, V_PARTS, W_PARTS = 2, 1, 1
F32 = jnp.float32
BF16 = jnp.bfloat16
SUBL = 8

VMEM = pl.BlockSpec(memory_space=pltpu.VMEM)
SMEM = pl.BlockSpec(memory_space=pltpu.SMEM)
HBM = pl.BlockSpec(memory_space=pltpu.HBM)


def dot(a, b):
    return jnp.dot(a, b, preferred_element_type=F32)


def onehot(shape, rows_to_cols):
    r = lax.broadcasted_iota(jnp.int32, shape, 0)
    c = lax.broadcasted_iota(jnp.int32, shape, 1)
    return jnp.where(rows_to_cols(r, c), 1.0, 0.0).astype(BF16)


def attention_kernel(
    n_chunks, len_hbm, q_hbm, nk_hbm, nv_hbm, res_hbm, k_hbm, v_hbm, wo_hbm,
    out_ref, len_ref, q_ref, nk_ref, nv_ref, res_ref, kbuf, vbuf, wobuf, sc_ref, w_ref, mix_ref,
    ho_ref, ssem, ksem, vsem, wsem,
):
    rows, heads, hd = q_ref.shape
    win = kbuf.shape[1]
    per = rows // n_chunks
    scale = 1.0 / math.sqrt(hd)

    def split(src, dst, first, n, parts, sems):
        step = n // parts
        return [
            pltpu.make_async_copy(
                src.at[pl.ds(first + i * step, step)], dst.at[pl.ds(first + i * step, step)], sems.at[i]
            )
            for i in range(parts)
        ]

    kcp = [split(k_hbm.at[:, 0], kbuf, c * per, per, K_PARTS, ksem.at[c]) for c in range(n_chunks)]
    vcp = [split(v_hbm.at[:, 0], vbuf, c * per, per, V_PARTS, vsem.at[c]) for c in range(n_chunks)]
    n_w = W_PARTS
    step_w = wobuf.shape[0] // n_w
    wcp = split(wo_hbm, wobuf, 0, wobuf.shape[0], n_w, wsem)
    small = [
        pltpu.make_async_copy(src, dst, ssem.at[i])
        for i, (src, dst) in enumerate(
            ((q_hbm, q_ref), (len_hbm, len_ref), (nk_hbm, nk_ref), (nv_hbm, nv_ref), (res_hbm, res_ref))
        )
    ]
    for cp in small + sum(kcp, []) + sum(vcp, []) + wcp:
        cp.start()
    for cp in small:
        cp.wait()

    q = q_ref[...].astype(F32)
    own = jnp.sum(q * nk_ref[...].astype(F32)[:, None, :], -1, keepdims=True) * scale
    new_v = nv_ref[...].astype(F32)
    slot = lax.broadcasted_iota(jnp.int32, (heads, win), 1)
    for c in range(n_chunks):
        for cp in kcp[c]:
            cp.wait()
        for b in range(c * per, (c + 1) * per):
            s = lax.dot_general(q_ref[b], kbuf[b], (((1,), (1,)), ((), ())), preferred_element_type=F32)
            sc_ref[b] = jnp.where(slot < len_ref[b], s * scale, -1e30)
    for c in range(n_chunks):
        r = pl.ds(c * per, per)
        sc = sc_ref[r]
        own_c = own[c * per : (c + 1) * per]
        top = jnp.maximum(jnp.max(sc, -1, keepdims=True), own_c)
        w = jnp.exp(sc - top)
        ow = jnp.exp(own_c - top)
        den = jnp.sum(w, -1, keepdims=True) + ow
        w_ref[r] = w.astype(BF16)
        owv = ow.astype(BF16).astype(F32) * new_v[c * per : (c + 1) * per, None, :]
        for cp in vcp[c]:
            cp.wait()
        for b in range(c * per, (c + 1) * per):
            i = b - c * per
            mix_ref[pl.ds(b * heads, heads)] = (dot(w_ref[b], vbuf[b]) + owv[i]) / den[i]

    dev_rows = rows // 2
    tail = dev_rows - SUBL
    order = [(0, SUBL), (dev_rows, SUBL), (SUBL, tail), (dev_rows + SUBL, tail)]
    for h in range(heads):
        at = 0
        for first, n in order:
            piece = mix_ref[pl.ds(first * heads + h, n, stride=heads), :]
            ho_ref[pl.ds(at, n), pl.ds(h * hd, hd)] = piece
            at += n
    ho = ho_ref[...].astype(BF16)
    acc = None
    for i in range(n_w):
        wcp[i].wait()
        piece = dot(ho[:, i * step_w : (i + 1) * step_w], wobuf[pl.ds(i * step_w, step_w)])
        acc = piece if acc is None else acc + piece
    out_ref[...] = acc
    sub = lax.axis_index("sub")
    res = res_ref[...].astype(F32)

    @pl.when(sub == 0)
    def _():
        out_ref[pl.ds(0, SUBL)] += res[:SUBL]
        out_ref[pl.ds(2 * SUBL, tail)] += res[SUBL:]

    @pl.when(sub == 1)
    def _():
        out_ref[pl.ds(SUBL, SUBL)] += res[:SUBL]
        out_ref[pl.ds(2 * SUBL + tail, tail)] += res[SUBL:]


def norm_kernel(experts, a_ref, b_ref, gain_ref, route_ref, rw_ref, _g, _u, _d, pay_ref, stream_ref, nrm_ref):
    rows, width = a_ref.shape
    dev_rows = rows // 2
    tail = dev_rows - SUBL
    cols = width // 2
    chunks = 2 * SUBL // (2 * tail)
    cw = cols // chunks
    s0 = lax.axis_index("sub") == 0
    stream = a_ref[...] + b_ref[...]
    mean = jnp.mean(stream * stream, -1, keepdims=True)
    normed = stream * lax.rsqrt(mean + 1e-06) * gain_ref[...]
    nrm_ref[...] = jnp.where(s0, normed[:, :cols], normed[:, cols:])
    main = nrm_ref[pl.ds(0, 2 * SUBL)]
    rest = nrm_ref[pl.ds(2 * SUBL, 2 * tail)]
    folded = jnp.concatenate([rest[:, c * cw : (c + 1) * cw] for c in range(chunks)], 0)
    pay_ref[:, pl.ds(0, cols)] = main.astype(BF16)
    pay_ref[:, pl.ds(cols, cw)] = folded.astype(BF16)
    stream_ref[pl.ds(0, SUBL)] = jnp.where(s0, stream[:SUBL], stream[SUBL : 2 * SUBL])
    stream_ref[pl.ds(SUBL, tail)] = jnp.where(
        s0, stream[2 * SUBL : 2 * SUBL + tail], stream[2 * SUBL + tail :]
    )
    lane = lax.broadcasted_iota(jnp.int32, (dev_rows, 2 * experts), 1)
    which = jnp.where(lane < experts, lane, lane - experts)
    route, rw = route_ref[...], rw_ref[...]
    dense = jnp.zeros((dev_rows, 2 * experts), F32)
    for k in range(route.shape[1]):
        dense += jnp.where(route[:, k : k + 1] == which, rw[:, k : k + 1], 0.0)
    high = dense.astype(BF16).astype(F32)
    pair = jnp.where(lane < experts, high, dense - high)
    pad = jnp.zeros((SUBL - tail, 2 * experts), F32)
    first = jnp.concatenate([pair[:SUBL], pair[SUBL:], pad], 0)
    second = jnp.concatenate([pair[SUBL:], pad, pair[:SUBL]], 0)
    pay_ref[:, pl.ds(cols + cw, 2 * experts)] = jnp.where(s0, first, second).astype(BF16)


def join_kernel(*refs):
    out_ref, at = refs[-1], 0
    for ref in refs[:-1]:
        n = ref.shape[0]
        out_ref[pl.ds(at, n)] = ref[...]
        at += n


def join(arrays):
    rows = sum(x.shape[0] for x in arrays)
    return pl.pallas_call(
        join_kernel,
        in_specs=[VMEM] * len(arrays),
        out_specs=VMEM,
        out_shape=jax.ShapeDtypeStruct((rows,) + arrays[0].shape[1:], arrays[0].dtype),
        compiler_params=params(4),
    )(*arrays)


def unpack_tokens(x_ref, piece_ref, cols, chunks, skip=0):
    br = piece_ref.shape[1]
    blocks = piece_ref.shape[0] - skip
    piece_ref = piece_ref.at[pl.ds(skip, blocks)]
    tail = br // chunks
    cw = cols // chunks
    x_ref[pl.ds(0, blocks * br)] = piece_ref[:, :, pl.ds(0, cols)].reshape(blocks * br, cols)
    folded = piece_ref[:, :, pl.ds(cols, cw)].reshape(blocks * br, cw)
    for c in range(chunks):
        pick = onehot(
            (blocks * tail, blocks * br),
            lambda r, q: q == (r // tail) * br + c * tail + r % tail,
        )
        x_ref[pl.ds(blocks * br, blocks * tail), pl.ds(c * cw, cw)] = dot(pick, folded).astype(BF16)


def first_half_kernel(chunks, skip, piece_ref, gate_ref, up_ref, g_ref, u_ref, x_ref):
    n, width, _ = gate_ref.shape
    cols = width // 2
    unpack_tokens(x_ref, piece_ref, cols, chunks, skip)
    at = pl.ds(pl.multiple_of(lax.axis_index("sub") * cols, cols), cols)
    for e in range(n):
        g_ref[e] = dot(x_ref[...], gate_ref[e, at, :])
        u_ref[e] = dot(x_ref[...], up_ref[e, at, :])


def second_half_kernel(
    chunks, oth_ref, ga_ref, ua_ref, gb_ref, ub_ref, gate_ref, up_ref, hid_ref, x_ref
):
    n, width, _ = gate_ref.shape
    cols = width // 2
    early = ga_ref.shape[1] * chunks // (chunks + 1)
    late = gb_ref.shape[1] * chunks // (chunks + 1)

    def whole(a, b):
        return jnp.concatenate([a[:early], b[:late], a[early:], b[late:]], 0)

    unpack_tokens(x_ref, oth_ref, cols, chunks)
    at = pl.ds(pl.multiple_of((1 - lax.axis_index("sub")) * cols, cols), cols)
    for e in range(n):
        gate = whole(ga_ref[e], gb_ref[e]) + dot(x_ref[...], gate_ref[e, at, :])
        up = whole(ua_ref[e], ub_ref[e]) + dot(x_ref[...], up_ref[e, at, :])
        hid_ref[e] = (gate / (1.0 + jnp.exp(-gate)) * up).astype(BF16)


def third_kernel(chunks, own_ref, oth_ref, hid_ref, down_ref, keep_ref, send_ref, acc_ref, comb_ref):
    n, _, width = down_ref.shape
    cols = width // 2
    blocks, br, wide = oth_ref.shape
    cw = cols // chunks
    experts = (wide - cols - cw) // 2
    tail = br // chunks
    sub = lax.axis_index("sub")
    s0 = sub == 0
    mine = own_ref[:, :, pl.ds(cols + cw, 2 * experts)]
    other = oth_ref[:, :, pl.ds(cols + cw, 2 * experts)]
    c0 = jnp.where(s0, mine, other)
    c1 = jnp.where(s0, other, mine)
    row = lax.broadcasted_iota(jnp.int32, c0.shape, 1)
    comb_ref[pl.ds(0, blocks * br)] = (
        jnp.where(row < SUBL, c0, c1).astype(F32).reshape(blocks * br, 2 * experts)
    )
    ht = tail // 2
    shape = (blocks * tail, blocks * br)
    pick0 = onehot(shape, lambda r, q: (r % tail < ht) & (q == (r // tail) * br + SUBL + r % tail))
    pick1 = onehot(shape, lambda r, q: (r % tail >= ht) & (q == (r // tail) * br + r % tail - ht))
    comb_ref[pl.ds(blocks * br, blocks * tail)] = dot(
        pick0, c0.reshape(blocks * br, 2 * experts)
    ) + dot(pick1, c1.reshape(blocks * br, 2 * experts))
    lane = lax.broadcasted_iota(jnp.int32, comb_ref.shape, 1)
    first_expert = (2 * lax.axis_index("ep") + sub) * n
    comb = comb_ref[...]
    for e in range(n):
        mine_e = (lane == first_expert + e) | (lane == first_expert + e + experts)
        weight = jnp.sum(jnp.where(mine_e, comb, 0.0), -1, keepdims=True)
        y = dot(hid_ref[e], down_ref[e]).astype(BF16).astype(F32) * weight
        acc_ref[...] = y if e == 0 else acc_ref[...] + y

    ow = width // (SUBL // ht)
    main = acc_ref[pl.ds(0, blocks * br)].reshape(blocks, 2, SUBL, width)
    m0, m1 = main[:, 0], main[:, 1]
    keep_ref[:, :, pl.ds(0, width)] = jnp.where(s0, m0, m1).astype(BF16)
    send_ref[:, :, pl.ds(0, width)] = jnp.where(s0, m1, m0).astype(BF16)
    rest = acc_ref[pl.ds(blocks * br, blocks * tail)].astype(BF16)
    for ref, side in ((keep_ref, sub), (send_ref, 1 - sub)):
        total = jnp.zeros((blocks * SUBL, ow), F32)
        for c in range(SUBL // ht):
            pick = onehot(
                (blocks * SUBL, blocks * tail),
                lambda r, q: ((r % SUBL) // ht == c) & (q == (r // SUBL) * tail + ht * side + r % ht),
            )
            total += dot(pick, rest[:, c * ow : (c + 1) * ow])
        ref[:, :, pl.ds(width, ow)] = total.reshape(blocks, SUBL, ow).astype(ref.dtype)


def finish_kernel(stream_ref, a_ref, b_ref, out_ref):
    dev_rows, width = stream_ref.shape
    tail = dev_rows - SUBL
    chunks = SUBL // tail
    total = a_ref[...] + b_ref[...].astype(F32)
    out_ref[pl.ds(0, SUBL)] = (stream_ref[pl.ds(0, SUBL)] + total[:, :width]).astype(BF16)
    rest = jnp.concatenate([total[c * tail : (c + 1) * tail, width:] for c in range(chunks)], 1)
    out_ref[pl.ds(SUBL, tail)] = (stream_ref[pl.ds(SUBL, tail)] + rest).astype(BF16)


def params(mib):
    return pltpu.CompilerParams(vmem_limit_bytes=mib << 20)


def layer(
    queries, cache_keys, cache_values, new_keys, new_values, lengths, out_proj, residual,
    norm_gain, gate_proj, up_proj, down_proj, routing, route_weights,
):
    rows, heads, hd = queries.shape
    in_hbm = functools.partial(pltpu.with_memory_space_constraint, memory_space=pltpu.HBM)
    raw = (gate_proj, up_proj, down_proj)
    in_vmem = functools.partial(pltpu.with_memory_space_constraint, memory_space=pltpu.VMEM)
    gate_proj, up_proj, down_proj = map(in_vmem, (gate_proj, up_proj, down_proj))
    win = cache_keys.shape[2]
    width = residual.shape[1]
    dev_rows = residual.shape[0]
    n_ep = lax.axis_size("ep")
    n_exp = gate_proj.shape[0]
    ff = gate_proj.shape[2]
    experts = n_exp * n_ep * lax.axis_size("sub")
    tail = dev_rows - SUBL
    cols = width // 2
    chunks = SUBL // tail
    cw = cols // chunks
    br = 2 * SUBL
    n_chunks = 2
    tokens = n_ep * rows
    swap = [(0, 1), (1, 0)]

    def to(x, m):
        return lax.ppermute(x, "ep", [(i, i ^ m) for i in range(n_ep)])

    partial = pl.pallas_call(
        functools.partial(attention_kernel, n_chunks),
        in_specs=[HBM] * 8,
        out_specs=VMEM,
        out_shape=jax.ShapeDtypeStruct((rows, width), F32),
        scratch_shapes=[
            pltpu.SMEM((rows,), jnp.int32),
            pltpu.VMEM(queries.shape, BF16),
            pltpu.VMEM((rows, hd), BF16),
            pltpu.VMEM((rows, hd), BF16),
            pltpu.VMEM(residual.shape, BF16),
            pltpu.VMEM((rows, win, hd), BF16),
            pltpu.VMEM((rows, win, hd), BF16),
            pltpu.VMEM(out_proj.shape, BF16),
            pltpu.VMEM((rows, heads, win), F32),
            pltpu.VMEM((rows, heads, win), BF16),
            pltpu.VMEM((rows * heads, hd), F32),
            pltpu.VMEM((rows, heads * hd), F32),
            pltpu.SemaphoreType.DMA((5,)),
            pltpu.SemaphoreType.DMA((n_chunks, K_PARTS)),
            pltpu.SemaphoreType.DMA((n_chunks, V_PARTS)),
            pltpu.SemaphoreType.DMA((W_PARTS,)),
        ],
        compiler_params=params(14),
        name="attention",
    )(
        *map(
            in_hbm,
            (
                lengths, queries, new_keys.reshape(rows, hd), new_values.reshape(rows, hd), residual,
                cache_keys, cache_values, out_proj,
            ),
        ),
    )

    from_sibling = lax.ppermute(partial, "sub", swap)
    payload, stream = pl.pallas_call(
        functools.partial(norm_kernel, experts),
        in_specs=[VMEM] * 5 + [HBM] * 3,
        out_specs=(VMEM, VMEM),
        out_shape=(
            jax.ShapeDtypeStruct((br, cols + cw + 2 * experts), BF16),
            jax.ShapeDtypeStruct((dev_rows, width), F32),
        ),
        scratch_shapes=[pltpu.VMEM((rows, cols), F32)],
        compiler_params=params(4),
        name="norm",
    )(partial, from_sibling, norm_gain.reshape(1, width), routing, route_weights, *map(in_hbm, raw))

    pieces = payload[None]
    far = []
    m = n_ep // 2
    while m >= 4:
        far.append(m)
        got = to(pieces, m)
        pieces = join([pieces, got])
        m //= 2
    near = list(range(1, min(4, n_ep)))
    early = pieces
    got = []
    for m in near:
        got.append(to(pieces, m))
    pieces = join([pieces] + got)
    others = lax.ppermute(pieces, "sub", swap)

    def first_half(x, skip):
        n_rows = (x.shape[0] - skip) * rows
        shape = jax.ShapeDtypeStruct((n_exp, n_rows, ff), F32)
        return pl.pallas_call(
            functools.partial(first_half_kernel, chunks, skip),
            in_specs=[VMEM] * 3,
            out_specs=(VMEM,) * 2,
            out_shape=(shape, shape),
            scratch_shapes=[pltpu.VMEM((n_rows, cols), BF16)],
            compiler_params=params(4),
        )(x, gate_proj, up_proj)

    gate_early, up_early = first_half(early, 0)
    gate_late, up_late = first_half(pieces, early.shape[0])

    hidden = pl.pallas_call(
        functools.partial(second_half_kernel, chunks),
        in_specs=[VMEM] * 7,
        out_specs=VMEM,
        out_shape=jax.ShapeDtypeStruct((n_exp, tokens, ff), BF16),
        scratch_shapes=[pltpu.VMEM((tokens, cols), BF16)],
        compiler_params=params(4),
        name="experts_second",
    )(others, gate_early, up_early, gate_late, up_late, gate_proj, up_proj)

    ow = width // chunks
    keep, send = pl.pallas_call(
        functools.partial(third_kernel, chunks),
        in_specs=[VMEM] * 4,
        out_specs=(VMEM, VMEM),
        out_shape=(
            jax.ShapeDtypeStruct((n_ep, SUBL, width + ow), BF16),
            jax.ShapeDtypeStruct((n_ep, SUBL, width + ow), BF16),
        ),
        scratch_shapes=[pltpu.VMEM((tokens, width), F32), pltpu.VMEM((tokens, 2 * experts), F32)],
        compiler_params=params(4),
        name="experts_third",
    )(pieces, others, hidden, down_proj)

    sums = keep.astype(F32) + lax.ppermute(send, "sub", swap).astype(F32)
    size = n_ep // (len(near) + 1)
    arrived = []
    for i, m in enumerate(near, 1):
        arrived.append(to(sums[i * size : (i + 1) * size].astype(BF16), m))
    sums = sums[:size]
    for x in arrived:
        sums = sums + x.astype(F32)
    last = None
    for m in reversed(far):
        size //= 2
        if last is not None:
            sums = sums + last.astype(F32)
        last = to(sums[size:].astype(BF16), m)
        sums = sums[:size]
    if last is None:
        last = jnp.zeros(sums.shape, BF16)

    return pl.pallas_call(
        finish_kernel,
        in_specs=[VMEM] * 3,
        out_specs=VMEM,
        out_shape=jax.ShapeDtypeStruct((dev_rows, width), BF16),
        compiler_params=params(4),
        name="finish",
    )(stream, sums[0], last[0])


def solution(mesh):
    return build(mesh)


def build(mesh):
    return jax.shard_map(
        layer,
        mesh=mesh,
        in_specs=(
            P(("grp", "ep"), "sub", None),
            P(("grp", "ep"), "sub", None, None),
            P(("grp", "ep"), "sub", None, None),
            P(("grp", "ep"), "sub", None),
            P(("grp", "ep"), "sub", None),
            P(("grp", "ep")),
            P("sub", None),
            P(("grp", "ep", "sub"), None),
            P(),
            P(("ep", "sub"), None, None),
            P(("ep", "sub"), None, None),
            P(("ep", "sub"), None, None),
            P(("grp", "ep", "sub"), None),
            P(("grp", "ep", "sub"), None),
        ),
        out_specs=P(("grp", "ep", "sub"), None),
        check_vma=False,
    )
```
